128 devices in a mesh: layer: 32 (over x_hi, y, z), dir: 4 (over x_lo, core).
Axes of the slice: x: 4 (x_hi: 2, x_lo: 2; x = x_hi * 2 + x_lo), y: 4, z: 4, core: 2. Of those that a mesh axis runs over, the one named last changes fastest.
Arguments:
- screens: bfloat16 [3, 2048, 16384], P(None, 'dir', 'layer'), may hold values from -6 to 6
- amplitude: float32 [1024, 1280], P('layer'), may hold values from 0.5 to 2
- wind: int32 [3, 2], replicated, may hold values from -8 to 8, as said below
- offsets: int32 [4, 3, 2], replicated, may hold values from 0 to 16383, as said below
- ratio: int32 [4, 3, 2], replicated, may hold values from 64 to 192, as said below
Outputs:
- new_screens: bfloat16 [3, 2048, 16384], P(None, 'dir', 'layer')
- spots: float32 [4, 2048, 2560], P('dir', 'layer')
The draws below stay inside these ranges and needn't reach their ends.
Inputs may be any that keep to these rules, and one draw needn't show every extreme that they name: wind[l, 0] is layer l's row shift and wind[l, 1] its column shift; no shift is zero; one layer has column shift +8 and a row shift above zero, another has column shift -8 and a row shift below zero. offsets[d, l, 0] is a screen row below 2048, offsets[d, l, 1] a screen column below 16384. ratio[d, l] = (num, den) with 64 <= den <= 128 and den <= num <= den + den // 2; some entry is (192, 128) and another (64, 64).
All inputs are finite; a program needn't handle non-finite values.
Results may differ from the reference program's by a relative error of at most 0.009.
Values may be sent and summed in bfloat16 or wider, within the bound.
A program may use at most 64 MiB of HBM per device.

```python
import math
import jax
import jax.numpy as jnp
from jax import lax

LAYERS = 3
SUB_PIX = 16
SPOT_PIX = 32
WIND_MAX = 8
DIRS = 4
PUPIL_ROWS = 1024
PUPIL_COLS = 1280
SCREEN_ROWS = 2048
SCREEN_COLS = 16384


def draw_wind(key, part):
    keys = jax.random.split(key, 4)
    layer_ids = jnp.arange(LAYERS, dtype=jnp.int32)
    sizes = jax.random.randint(keys[0], (LAYERS, 2), 1, WIND_MAX + 1)
    signs = jax.random.randint(keys[1], (LAYERS, 2), 0, 2) * 2 - 1
    first = jax.random.randint(keys[2], (), 0, LAYERS)
    second = (first + jax.random.randint(keys[3], (), 1, LAYERS)) % LAYERS
    moves = sizes * signs
    forced = jnp.where(layer_ids == first, 1, jnp.where(layer_ids == second, -1, 0))
    row_moves = jnp.where(forced != 0, forced * sizes[:, 0], moves[:, 0])
    col_moves = jnp.where(forced != 0, forced * WIND_MAX, moves[:, 1])
    return jnp.stack([row_moves, col_moves], axis=1).astype(jnp.int32)


def draw_offsets(key, part):
    keys = jax.random.split(key, 5)
    rows = jax.random.randint(keys[0], (DIRS, LAYERS), 0, SCREEN_ROWS)
    cols = jax.random.randint(keys[1], (DIRS, LAYERS), 0, SCREEN_COLS)
    entries = DIRS * LAYERS
    flat = jnp.arange(entries, dtype=jnp.int32).reshape(DIRS, LAYERS)
    top_row = jax.random.randint(keys[2], (), 0, entries)
    zero_row = (top_row + jax.random.randint(keys[3], (), 1, entries)) % entries
    top_col = jax.random.randint(keys[4], (), 0, entries)
    rows = jnp.where(flat == top_row, SCREEN_ROWS - 1, rows)
    rows = jnp.where(flat == zero_row, 0, rows)
    cols = jnp.where(flat == top_col, SCREEN_COLS - 1, cols)
    return jnp.stack([rows, cols], axis=2).astype(jnp.int32)


def draw_ratio(key, part):
    keys = jax.random.split(key, 4)
    denoms = jax.random.randint(keys[0], (DIRS, LAYERS), 64, 129)
    extra = jax.random.randint(keys[1], (DIRS, LAYERS), 0, 65) % (denoms // 2 + 1)
    entries = DIRS * LAYERS
    flat = jnp.arange(entries, dtype=jnp.int32).reshape(DIRS, LAYERS)
    top_entry = jax.random.randint(keys[2], (), 0, entries)
    low_entry = (top_entry + jax.random.randint(keys[3], (), 1, entries)) % entries
    denoms = jnp.where(flat == top_entry, 128, jnp.where(flat == low_entry, 64, denoms))
    extra = jnp.where(flat == top_entry, 64, jnp.where(flat == low_entry, 0, extra))
    return jnp.stack([denoms + extra, denoms], axis=2).astype(jnp.int32)


def shard_levels(rng, dims, pieces, smallest, high):
    def one(axis_at, parts):
        steps = jax.random.uniform(jax.random.fold_in(jax.random.fold_in(rng, 6), axis_at), (parts,), jnp.float32, smallest / len(pieces), high / len(pieces))
        return jnp.repeat(jnp.exp(steps), dims[axis_at] // parts).reshape((-1,) + (1,) * (len(dims) - axis_at - 1))

    level = one(*pieces[0])
    for cut in pieces[1:]:
        level = level * one(*cut)
    return level


def noise(stream_key, extent, scale, most, shards=(), held_as=jnp.bfloat16):
    values = scale * jax.random.normal(stream_key, extent, jnp.float32)
    if shards:
        values = values * shard_levels(stream_key, extent, shards, -0.22, 0.18)
    return jnp.clip(values, -most, most).astype(held_as)


def setup_inputs(seed: int = 0) -> dict:
    splits = jax.random.split(jax.random.key(seed), 6)
    screens = noise(splits[0], (LAYERS, SCREEN_ROWS, SCREEN_COLS), 1.0, 6.0, ((1, 4), (2, 32)))
    amplitude = jnp.clip(jnp.exp(math.log(2.0) - 1.3862944 * jax.random.uniform(splits[1], (PUPIL_ROWS, PUPIL_COLS), jnp.float32) ** shard_levels(splits[1], (PUPIL_ROWS, PUPIL_COLS), ((0, 32),), -0.2, 0.2)), 0.5, 2.0)
    wind = draw_wind(jax.random.fold_in(splits[5], 71), 0)
    offsets = draw_offsets(jax.random.fold_in(splits[5], 71), 0)
    ratio = draw_ratio(jax.random.fold_in(splits[5], 71), 0)
    return {"screens": screens, "amplitude": amplitude, "wind": wind, "offsets": offsets, "ratio": ratio}


def spans(anchor, stretch_num, stretch_den, count, length):
    pixel = jnp.arange(count, dtype=jnp.int32)
    stretched = pixel * stretch_num
    base = (anchor + stretched // stretch_den) % length
    upper = (base + 1) % length
    fraction = (stretched % stretch_den).astype(jnp.float32) / stretch_den.astype(jnp.float32)
    return base, upper, (1.0 - fraction).astype(jnp.bfloat16), fraction.astype(jnp.bfloat16)


def dft_tables():
    freq = jnp.arange(SPOT_PIX, dtype=jnp.int32)[:, None] - SPOT_PIX // 2
    pixel = jnp.arange(SUB_PIX, dtype=jnp.int32)[None, :]
    turns = (freq * pixel) % SPOT_PIX
    angle = turns.astype(jnp.float32) * (2.0 * jnp.pi / SPOT_PIX)
    return jnp.cos(angle), -jnp.sin(angle)


def imaging(phase, amplitude):
    rows, cols = phase.shape
    sub_rows = rows // SUB_PIX
    sub_cols = cols // SUB_PIX
    real = (amplitude * jnp.cos(phase)).reshape(sub_rows, SUB_PIX, sub_cols, SUB_PIX)
    imag = (amplitude * jnp.sin(phase)).reshape(sub_rows, SUB_PIX, sub_cols, SUB_PIX)
    cos_table, sin_table = dft_tables()
    highest = lax.Precision.HIGHEST
    half_real = jnp.einsum('aibj,kj->aibk', real, cos_table, precision=highest) - jnp.einsum('aibj,kj->aibk', imag, sin_table, precision=highest)
    half_imag = jnp.einsum('aibj,kj->aibk', real, sin_table, precision=highest) + jnp.einsum('aibj,kj->aibk', imag, cos_table, precision=highest)
    full_real = jnp.einsum('ki,aibl->akbl', cos_table, half_real, precision=highest) - jnp.einsum('ki,aibl->akbl', sin_table, half_imag, precision=highest)
    full_imag = jnp.einsum('ki,aibl->akbl', cos_table, half_imag, precision=highest) + jnp.einsum('ki,aibl->akbl', sin_table, half_real, precision=highest)
    intensity = full_real * full_real + full_imag * full_imag
    totals = jnp.sum(intensity, axis=(1, 3), keepdims=True)
    normed = intensity * float(SPOT_PIX * SPOT_PIX) / totals
    return normed.reshape(sub_rows * SPOT_PIX, sub_cols * SPOT_PIX)


def reference(screens, amplitude, wind, offsets, ratio):
    moved = jnp.stack([jnp.roll(screens[k], (wind[k, 0], wind[k, 1]), axis=(0, 1)) for k in range(LAYERS)])
    spot_list = []
    for direction in range(DIRS):
        phase = jnp.zeros((PUPIL_ROWS, PUPIL_COLS), jnp.float32)
        for k in range(LAYERS):
            stretch_num = ratio[direction, k, 0]
            stretch_den = ratio[direction, k, 1]
            row_base, row_upper, row_low, row_high = spans(offsets[direction, k, 0], stretch_num, stretch_den, PUPIL_ROWS, SCREEN_ROWS)
            screen = moved[k].astype(jnp.float32)
            projected = row_low.astype(jnp.float32)[:, None] * screen[row_base] + row_high.astype(jnp.float32)[:, None] * screen[row_upper]
            projected = lax.optimization_barrier(projected.astype(jnp.bfloat16)).astype(jnp.float32)
            col_base, col_upper, col_low, col_high = spans(offsets[direction, k, 1], stretch_num, stretch_den, PUPIL_COLS, SCREEN_COLS)
            phase = phase + (projected[:, col_base] * col_low.astype(jnp.float32)[None, :] + projected[:, col_upper] * col_high.astype(jnp.float32)[None, :])
        spot_list.append(imaging(phase, amplitude))
    return moved, jnp.stack(spot_list)
```

```python
import functools

import jax
import jax.numpy as jnp
import numpy as np
from jax import lax
from jax.experimental import pallas as pl
from jax.experimental.pallas import tpu as pltpu
from jax.sharding import PartitionSpec as P

MESH = pl.DeviceIdType.MESH
SUB = 16
SPOT = 32
HALO = 8
LAYERS = 3
DIRS = 4
ROWS, COLS = 2048, 16384
PR, PC = 1024, 1280
BLK = 512
CHIPS = 64
JT = PC // 128
NPR = 32
F32, BF16, I32 = jnp.float32, jnp.bfloat16, jnp.int32
HIGHEST = lax.Precision.HIGHEST


def iota(shape, dim):
    return lax.broadcasted_iota(I32, shape, dim)


def floor_div(a, den):
    q = jnp.floor(a / den)
    r = a - q * den
    q = q + jnp.where(r >= den, 1.0, 0.0) - jnp.where(r < 0.0, 1.0, 0.0)
    return q


def reciprocals():
    den = np.maximum(np.arange(129), 1)
    return (2 ** 21 // den + 1).astype(np.int32)


def stretch(i, unit, num, den, mul):
    part = i * (num - den)
    whole = (part * mul) >> 21
    rest = part - whole * den
    return unit * (i + whole) + ((unit * rest * mul) >> 21)


def sincos(x):
    n = jnp.floor(x * np.float32(2.0 / np.pi) + 0.5)
    r = x - n * np.float32(1.5703125)
    r = r - n * np.float32(4.837512969970703125e-4)
    r = r - n * np.float32(7.54978995489188216e-8)
    r2 = r * r
    s = r + r * r2 * (
        np.float32(-1.6666654611e-1)
        + r2 * (np.float32(8.3321608736e-3) + r2 * np.float32(-1.9515295891e-4))
    )
    c = (
        1.0
        - 0.5 * r2
        + r2 * r2 * (
            np.float32(4.166664568298827e-2)
            + r2 * (np.float32(-1.388731625493765e-3) + r2 * np.float32(2.443315711809948e-5))
        )
    )
    k = n.astype(I32)
    swap = (k & 1) == 1
    sin = jnp.where(swap, c, s)
    cos = jnp.where(swap, s, c)
    sin = jnp.where((k & 2) == 2, -sin, sin)
    cos = jnp.where(((k + 1) & 2) == 2, -cos, cos)
    return sin, cos


def dft_tables():
    turns = ((np.arange(SPOT)[:, None] - SPOT // 2) * np.arange(SUB)[None, :]) % SPOT
    angle = turns * (2.0 * np.pi / SPOT)
    c, s = np.cos(angle), -np.sin(angle)
    cols = np.concatenate([np.kron(np.eye(8), c.T), np.kron(np.eye(8), s.T)], axis=1)
    cb, sb = np.kron(np.eye(2), c), np.kron(np.eye(2), s)
    rows = np.block([[cb, -sb], [sb, cb]])
    return cols.astype(np.float32), rows.astype(np.float32)


def shift_at(x, k):
    b, xl = x
    px = ((b // 16) * 2 + xl + k % 4) % 4
    py = ((b // 4) % 4 + (k // 4) % 4) % 4
    pz = (b % 4 + k // 16) % 4
    return (px // 2) * 16 + py * 4 + pz, px % 2


def kernel(
    wind, offs, ratio, magic, screens, amp, dcol, drow,
    new_out, spots,
    x, send1, recv_a, recv_b, recv_c, halo_s, halo_r, edge_s, edge_r, y,
    relb, frac, d_buf, e_buf, stage, send2, recv2, wrow, wbig, ampn, field,
    in_sem, s1, r1, hs, hr, es, er, ws, wr, s2, r2, osem, round2,
):
    recv1 = (recv_a, recv_b, recv_c)
    b = lax.axis_index("layer")
    q = lax.axis_index("dir")
    xl, c = q // 2, q % 2
    chip = b * 2 + xl

    def device(pb, pxl):
        return (pb, pxl * 2 + c)

    bar = pltpu.get_barrier_semaphore()

    up = (b, (q + 1) % 4)
    down = (b, (q + 3) % 4)
    right = ((b + 1) % 32, q)
    left = ((b + 31) % 32, q)

    loads = [pltpu.make_async_copy(screens.at[l], x.at[l], in_sem.at[l]) for l in range(LAYERS)]
    for load in loads:
        load.start()
    for dev in (up, down):
        pl.semaphore_signal(bar, inc=1, device_id=dev, device_id_type=MESH)

    def greet(k, _):
        pl.semaphore_signal(bar, inc=1, device_id=device(*group(b, xl, k, 0)), device_id_type=MESH)
        pl.semaphore_signal(bar, inc=1, device_id=device(*group(b, xl, k, 1)), device_id_type=MESH)
        return 0

    lax.fori_loop(1, 8, greet, 0)

    ro, ri = iota((BLK, BLK), 0), iota((BLK, BLK), 1)
    perm = jnp.where(ri == (ro & 7) * 64 + (ro >> 3), 1.0, 0.0).astype(BF16)

    pl.semaphore_wait(bar, 16)

    def greet2(k, _):
        pl.semaphore_signal(round2, inc=1, device_id=device(*group(b, xl, k, 1)), device_id_type=MESH)
        return 0

    lax.fori_loop(1, 8, greet2, 0)

    def permute(l):
        loads[l].wait()
        rows = jnp.dot(perm, x[l], preferred_element_type=F32)
        for t in range(4):
            send1[l, :, t] = rows[:, t * 128:(t + 1) * 128].reshape(CHIPS, 8, 128).astype(BF16)

    def exchange(l):
        def go(k, _):
            pb, pxl = shift_at((b, xl), k)
            pltpu.make_async_remote_copy(
                src_ref=send1.at[l, pb * 2 + pxl],
                dst_ref=recv1[l].at[xl, pl.ds(b * 4, 4)],
                send_sem=s1.at[l], recv_sem=r1.at[l],
                device_id=device(pb, pxl), device_id_type=MESH,
            ).start()
            return 0

        lax.fori_loop(1, CHIPS, go, 0)
        pltpu.make_async_copy(send1.at[l, chip], recv1[l].at[xl, pl.ds(b * 4, 4)], r1.at[l]).start()

    permute(0)
    pl.semaphore_wait(round2, 7)
    exchange(0)
    permute(1)
    exchange(1)
    permute(2)
    exchange(2)

    pick = (iota((8, 128), 0), iota((8, 128), 1))
    first = jnp.where(pick[1] == pick[0], 1.0, 0.0).astype(BF16)
    last = jnp.where(pick[1] == pick[0] + 120, 1.0, 0.0).astype(BF16)
    nt = (((1,), (1,)), ((), ()))
    for l in range(LAYERS):
        halo_s[0, l] = lax.dot_general(
            last, x[l, :, BLK - 128:], nt, preferred_element_type=F32).astype(BF16)
        halo_s[1, l] = lax.dot_general(
            first, x[l, :, :128], nt, preferred_element_type=F32).astype(BF16)
    halos = [
        pltpu.make_async_remote_copy(
            src_ref=halo_s.at[i], dst_ref=halo_r.at[i], send_sem=hs.at[i], recv_sem=hr.at[i],
            device_id=dev, device_id_type=MESH)
        for i, dev in enumerate((right, left))
    ]
    for h in halos:
        h.start()

    px0 = (iota((16, 128), 0) * 128).astype(F32)
    px = px0 + iota((16, 128), 1).astype(F32)
    for d in range(DIRS):
        for l in range(LAYERS):
            num = ratio[d, l, 0].astype(F32)
            den = ratio[d, l, 1].astype(F32)
            start = (offs[d, l, 1] - wind[l, 1] + COLS) & (COLS - 1)
            a = px * num
            qv = floor_div(a, den)
            tile = (start + floor_div(px0 * num, den).astype(I32)) >> 7
            relb[d * LAYERS + l] = start + qv.astype(I32) - tile * 128
            frac[d * LAYERS + l] = (a - qv * den) / den

    cc = iota((NPR, CHIPS * 32), 1)
    mrow, lj = cc >> 5, cc & 31
    lay = jnp.where(lj >= 20, 2, jnp.where(lj >= 10, 1, 0))
    lane_tile = lj - lay * 10
    weights = jnp.zeros((NPR, CHIPS * 32), F32)
    pupil = (b * NPR + iota((NPR, 1), 0)).astype(F32)
    for l in range(LAYERS):
        num = ratio[q, l, 0].astype(F32)
        den = ratio[q, l, 1].astype(F32)
        start = (offs[q, l, 0] - wind[l, 0] + ROWS) & (ROWS - 1)
        a = pupil * num
        qv = floor_div(a, den)
        f = (a - qv * den) / den
        base = (start + qv.astype(I32)) & 63
        high = f.astype(BF16).astype(F32)
        low = (1.0 - f).astype(BF16).astype(F32)
        w = jnp.where(mrow == base, low, 0.0) + jnp.where(mrow == ((base + 1) & 63), high, 0.0)
        weights = weights + jnp.where((lay == l) & (lane_tile < 10), w, 0.0)
    wrow[...] = weights
    for j in range(JT):
        wbig[j * NPR:(j + 1) * NPR] = jnp.where(lane_tile == j, wrow[...], 0.0).astype(BF16)

    g32 = jnp.where((iota((32, 32), 0) >> 4) == (iota((32, 32), 1) >> 4), 1.0, 0.0)
    g128 = jnp.where((iota((128, 128), 0) >> 4) == (iota((128, 128), 1) >> 4), 1.0, 0.0)
    for j in range(JT):
        av = amp[:, j * 128:(j + 1) * 128]
        energy = jnp.dot(g32, av * av, precision=HIGHEST, preferred_element_type=F32)
        energy = jnp.dot(energy, g128, precision=HIGHEST, preferred_element_type=F32)
        ampn[j] = av / jnp.sqrt(energy)

    stage[...] = jnp.zeros_like(stage)

    for h in halos:
        h.wait()
    tn = (((0,), (0,)), ((), ()))
    hr_i, hr_c = iota((8, BLK), 0), iota((8, BLK), 1)
    for l in range(LAYERS):
        w1 = wind[l, 1]
        main = jnp.where(ro == ri - w1, 1.0, 0.0).astype(BF16)
        left_m = jnp.where(hr_i - 8 == hr_c - w1, 1.0, 0.0).astype(BF16)
        right_m = jnp.where(hr_i + BLK == hr_c - w1, 1.0, 0.0).astype(BF16)
        val = jnp.dot(x[l], main, preferred_element_type=F32)
        val = val + lax.dot_general(halo_r[0, l], left_m, tn, preferred_element_type=F32)
        val = val + lax.dot_general(halo_r[1, l], right_m, tn, preferred_element_type=F32)
        y[l] = val.astype(BF16)
        edge_s[0, l] = val[BLK - 8:].astype(BF16)
        edge_s[1, l] = val[:8].astype(BF16)
    edges = [
        pltpu.make_async_remote_copy(
            src_ref=edge_s.at[i], dst_ref=edge_r.at[i], send_sem=es.at[i], recv_sem=er.at[i],
            device_id=dev, device_id_type=MESH)
        for i, dev in enumerate((up, down))
    ]
    for e in edges:
        e.start()

    def columns(l):
        def one(i, _):
            d, j = i // JT, i % JT
            num, den = ratio[d, l, 0], ratio[d, l, 1]
            start = (offs[d, l, 1] - wind[l, 1] + COLS) & (COLS - 1)
            tile = (start + stretch(j, 128, num, den, magic[den])) >> 7
            rel = relb[d * LAYERS + l, pl.ds(j, 1), :]
            f = frac[d * LAYERS + l, pl.ds(j, 1), :]
            high = f.astype(BF16).astype(F32)
            low = (1.0 - f).astype(BF16).astype(F32)
            rel = jnp.broadcast_to(rel, (8, 128))
            rel_u = rel + 1
            idx, idx_u = rel & 127, rel_u & 127
            sel, sel_u = rel >> 7, rel_u >> 7
            for h in range(2):
                t = [recv1[l][h, (tile + s) & 127].astype(F32) for s in range(3)]
                g = [jnp.take_along_axis(v, idx, axis=1) for v in t]
                u = [jnp.take_along_axis(v, idx_u, axis=1) for v in t]
                vb = jnp.where(sel == 0, g[0], jnp.where(sel == 1, g[1], g[2]))
                vu = jnp.where(sel_u == 0, u[0], jnp.where(sel_u == 1, u[1], u[2]))
                out = low * vb + high * vu
                e_buf.at[d % 2, l, d // 2, h].reshape(128, 128)[pl.ds(j, 8, stride=16), :] = out
            return 0

        lax.fori_loop(0, DIRS * JT, one, 0)

    def swap(l):
        return pltpu.make_async_remote_copy(
            src_ref=e_buf.at[1 - c, l], dst_ref=d_buf.at[l], send_sem=ws.at[l], recv_sem=wr.at[l],
            device_id=(b, xl * 2 + 1 - c), device_id_type=MESH)

    for l in range(LAYERS):
        pltpu.make_async_copy(recv1[l], recv1[l], r1.at[l]).wait()
        columns(l)
        swap(l).start()
        if l == 0:
            for e in edges:
                e.wait()
            for k in range(LAYERS):
                w0 = wind[k, 0]
                main = jnp.where(ri == ro - w0, 1.0, 0.0).astype(BF16)
                er_r, er_i = iota((BLK, 8), 0), iota((BLK, 8), 1)
                top_m = jnp.where(er_i - 8 == er_r - w0, 1.0, 0.0).astype(BF16)
                bot_m = jnp.where(er_i + BLK == er_r - w0, 1.0, 0.0).astype(BF16)
                val = jnp.dot(main, y[k], preferred_element_type=F32)
                val = val + jnp.dot(top_m, edge_r[0, k], preferred_element_type=F32)
                val = val + jnp.dot(bot_m, edge_r[1, k], preferred_element_type=F32)
                x[k] = val.astype(BF16)
                pltpu.make_async_copy(x.at[k], new_out.at[k], osem.at[k]).start()

    for l in range(LAYERS):
        swap(l).wait()

    def send_rows(p, _):
        for pxl in range(2):
            for l in range(LAYERS):
                num, den = ratio[pxl * 2 + c, l, 0], ratio[pxl * 2 + c, l, 1]
                s = (offs[pxl * 2 + c, l, 0] - wind[l, 0] + ROWS + stretch(p, NPR, num, den, magic[den])) & (ROWS - 1)
                row = (s + ((chip - s) & 63)) & (ROWS - 1)
                k = row >> 6
                h, cs, kk = k >> 4, (k >> 3) & 1, k & 7
                mine = e_buf[c, l, pxl, h, kk]
                other = d_buf[l, pxl, h, kk]
                keep = jnp.where(cs == c, 1, 0)
                val = jnp.where(jnp.broadcast_to(keep, (16, 128)) == 1, mine, other)
                stage[pxl, l * 10:l * 10 + 10, :] = val[:10]
            send2[p * 2 + pxl] = stage[pxl].astype(BF16)
        return 0

    lax.fori_loop(0, 32, send_rows, 0)

    def go2(k, _):
        pb, pxl = shift_at((b, xl), k)
        pltpu.make_async_remote_copy(
            src_ref=send2.at[pb * 2 + pxl], dst_ref=recv2.at[chip],
            send_sem=s2, recv_sem=r2,
            device_id=device(pb, pxl), device_id_type=MESH,
        ).start()
        return 0

    lax.fori_loop(1, CHIPS, go2, 0)
    pltpu.make_async_copy(send2.at[chip], recv2.at[chip], r2).start()
    pltpu.make_async_copy(recv2, recv2, r2).wait()

    phase = jnp.dot(wbig[...], recv2[...].reshape(CHIPS * 32, 128), preferred_element_type=F32)
    for j in range(JT):
        sin, cos = sincos(phase[j * NPR:(j + 1) * NPR])
        field[0, j] = ampn[j] * cos
        field[1, j] = ampn[j] * sin
    for j in range(JT):
        both = jnp.concatenate([field[0, j], field[1, j]], axis=0)
        g = jnp.dot(both, dcol[...], precision=HIGHEST, preferred_element_type=F32)
        half_re = g[:32, :256] - g[32:, 256:]
        half_im = g[:32, 256:] + g[32:, :256]
        half = jnp.concatenate([half_re, half_im], axis=0)
        full = jnp.dot(drow[...], half, precision=HIGHEST, preferred_element_type=F32)
        spots[:, j * 256:(j + 1) * 256] = full[:64] * full[:64] + full[64:] * full[64:]

    for l in range(LAYERS):
        pltpu.make_async_copy(send1.at[l, 0:63], send1.at[l, 0:63], s1.at[l]).wait()
        pltpu.make_async_copy(x.at[l], new_out.at[l], osem.at[l]).wait()
    pltpu.make_async_copy(send2.at[0:63], send2.at[0:63], s2).wait()


def group(b, xl, k, axis):
    xh, y, z = b // 16, (b // 4) % 4, b % 4
    if axis == 0:
        pos = (xl * 4 + z + k) % 8
        return xh * 16 + y * 4 + pos % 4, pos // 4
    pos = (xh * 4 + y + k) % 8
    return (pos // 4) * 16 + (pos % 4) * 4 + z, xl


def per_device(screens, amplitude, wind, offsets, ratio):
    cols, rows = dft_tables()
    vmem = pl.BlockSpec(memory_space=pltpu.VMEM)
    smem = pl.BlockSpec(memory_space=pltpu.SMEM)
    hbm = pl.BlockSpec(memory_space=pl.ANY)
    dma, reg = pltpu.SemaphoreType.DMA, pltpu.SemaphoreType.REGULAR
    new, spots = pl.pallas_call(
        kernel,
        out_shape=(
            jax.ShapeDtypeStruct((LAYERS, BLK, BLK), BF16),
            jax.ShapeDtypeStruct((64, 2560), F32),
        ),
        in_specs=[smem, smem, smem, smem, hbm, vmem, vmem, vmem],
        out_specs=(hbm, vmem),
        scratch_shapes=[
            pltpu.VMEM((LAYERS, BLK, BLK), BF16),
            pltpu.VMEM((LAYERS, CHIPS, 4, 8, 128), BF16),
            pltpu.VMEM((2, 128, 8, 128), BF16),
            pltpu.VMEM((2, 128, 8, 128), BF16),
            pltpu.VMEM((2, 128, 8, 128), BF16),
            pltpu.VMEM((2, LAYERS, 8, BLK), BF16),
            pltpu.VMEM((2, LAYERS, 8, BLK), BF16),
            pltpu.VMEM((2, LAYERS, 8, BLK), BF16),
            pltpu.VMEM((2, LAYERS, 8, BLK), BF16),
            pltpu.VMEM((LAYERS, BLK, BLK), BF16),
            pltpu.VMEM((DIRS * LAYERS, 16, 128), I32),
            pltpu.VMEM((DIRS * LAYERS, 16, 128), F32),
            pltpu.VMEM((LAYERS, 2, 2, 8, 16, 128), F32),
            pltpu.VMEM((2, LAYERS, 2, 2, 8, 16, 128), F32),
            pltpu.VMEM((2, 32, 128), F32),
            pltpu.VMEM((CHIPS, 32, 128), BF16),
            pltpu.VMEM((CHIPS, 32, 128), BF16),
            pltpu.VMEM((NPR, CHIPS * 32), F32),
            pltpu.VMEM((JT * NPR, CHIPS * 32), BF16),
            pltpu.VMEM((JT, NPR, 128), F32),
            pltpu.VMEM((2, JT, NPR, 128), F32),
            dma((3,)), dma((3,)), dma((3,)), dma((2,)), dma((2,)), dma((2,)), dma((2,)),
            dma((3,)), dma((3,)), dma, dma, dma((3,)), reg,
        ],
        compiler_params=pltpu.CompilerParams(
            collective_id=0, has_side_effects=True, vmem_limit_bytes=48 << 20),
        name="screens_to_spots",
    )(wind, offsets, ratio, jnp.asarray(reciprocals()), screens, amplitude, jnp.asarray(cols), jnp.asarray(rows))
    return new, spots[None]


def solution(mesh):
    return jax.shard_map(
        per_device,
        mesh=mesh,
        in_specs=(P(None, "dir", "layer"), P("layer", None), P(), P(), P()),
        out_specs=(P(None, "dir", "layer"), P("dir", "layer", None)),
        check_vma=False,
    )
```

```python
import jax
import jax.numpy as jnp
import numpy as np
from jax import lax
from jax.experimental import pallas as pl
from jax.experimental.pallas import tpu as pltpu
from jax.sharding import PartitionSpec as P

MESH = pl.DeviceIdType.MESH
SUB = 16
SPOT = 32
HALO = 8
LAYERS = 3
DIRS = 4
ROWS, COLS = 2048, 16384
PR, PC = 1024, 1280
BLK = 512
CHIPS = 64
JT = PC // 128
NPR = 32
F32, BF16, I32 = jnp.float32, jnp.bfloat16, jnp.int32
HIGHEST = lax.Precision.HIGHEST


def iota(shape, dim):
    return lax.broadcasted_iota(I32, shape, dim)


def floor_div(a, den):
    q = jnp.floor(a / den)
    r = a - q * den
    q = q + jnp.where(r >= den, 1.0, 0.0) - jnp.where(r < 0.0, 1.0, 0.0)
    return q


def reciprocals():
    den = np.maximum(np.arange(129), 1)
    return (2 ** 21 // den + 1).astype(np.int32)


def stretch(i, unit, num, den, mul):
    part = i * (num - den)
    whole = (part * mul) >> 21
    rest = part - whole * den
    return unit * (i + whole) + ((unit * rest * mul) >> 21)


def sincos(x):
    n = jnp.floor(x * np.float32(2.0 / np.pi) + 0.5)
    r = x - n * np.float32(1.5703125)
    r = r - n * np.float32(4.837512969970703125e-4)
    r = r - n * np.float32(7.54978995489188216e-8)
    r2 = r * r
    s = r + r * r2 * (
        np.float32(-1.6666654611e-1)
        + r2 * (np.float32(8.3321608736e-3) + r2 * np.float32(-1.9515295891e-4))
    )
    c = (
        1.0
        - 0.5 * r2
        + r2 * r2 * (
            np.float32(4.166664568298827e-2)
            + r2 * (np.float32(-1.388731625493765e-3) + r2 * np.float32(2.443315711809948e-5))
        )
    )
    k = n.astype(I32)
    swap = (k & 1) == 1
    sin = jnp.where(swap, c, s)
    cos = jnp.where(swap, s, c)
    sin = jnp.where((k & 2) == 2, -sin, sin)
    cos = jnp.where(((k + 1) & 2) == 2, -cos, cos)
    return sin, cos


def dft_tables():
    turns = ((np.arange(SPOT)[:, None] - SPOT // 2) * np.arange(SUB)[None, :]) % SPOT
    angle = turns * (2.0 * np.pi / SPOT)
    c, s = np.cos(angle), -np.sin(angle)
    cols = np.concatenate([np.kron(np.eye(8), c.T), np.kron(np.eye(8), s.T)], axis=1)
    cb, sb = np.kron(np.eye(2), c), np.kron(np.eye(2), s)
    rows = np.block([[cb, -sb], [sb, cb]])
    return cols.astype(np.float32), rows.astype(np.float32)


def shift_at(b, xl, k):
    px = ((b >> 4) * 2 + xl + (k & 3)) & 3
    py = ((b >> 2) + (k >> 2)) & 3
    pz = (b + (k >> 4)) & 3
    return (px >> 1) * 16 + py * 4 + pz, px & 1


def kernel(
    wind, offs, ratio, magic, screens, amp_h, dcol_h, drow_h,
    new_out, spots,
    x, amp, dcol, drow, send1, recv_a, recv_b, recv_c, halo_s, halo_r, edge_s, edge_r, y,
    relb, frac, b_a, b_b, b_c, send2a, send2b, recv2a, recv2b, wbig_a, wbig_b, ampn, phase, field,
    in_sem, tab_sem, s1, r1, hs, hr, es, er, ws, wr, s2, r2, osem,
):
    recv1, cols = (recv_a, recv_b, recv_c), (b_a, b_b, b_c)
    b = lax.axis_index("layer")
    q = lax.axis_index("dir")
    xl, c = q // 2, q % 2
    chip = b * 2 + xl

    def device(pb, pxl):
        return (pb, pxl * 2 + c)

    up = (b, (q + 1) % 4)
    down = (b, (q + 3) % 4)
    right = ((b + 1) % 32, q)
    left = ((b + 31) % 32, q)
    bar = pltpu.get_barrier_semaphore()
    for dev in (up, down):
        pl.semaphore_signal(bar, inc=1, device_id=dev, device_id_type=MESH)

    def greet(k, _):
        pl.semaphore_signal(bar, inc=1, device_id=device(*shift_at(b, xl, 64 - k)), device_id_type=MESH)
        return 0

    lax.fori_loop(1, CHIPS, greet, 0)

    loads = [pltpu.make_async_copy(screens.at[l], x.at[l], in_sem.at[l]) for l in range(LAYERS)]
    tables = [
        pltpu.make_async_copy(src, dst, tab_sem.at[i])
        for i, (src, dst) in enumerate(((amp_h, amp), (dcol_h, dcol), (drow_h, drow)))
    ]
    for load in loads + tables:
        load.start()

    ro, ri = iota((BLK, BLK), 0), iota((BLK, BLK), 1)
    perm = jnp.where(ri == (ro & 7) * 64 + (ro >> 3), 1.0, 0.0).astype(BF16)

    def permute(l):
        loads[l].wait()
        rows = jnp.dot(perm, x[l], preferred_element_type=F32)
        for t in range(4):
            send1[l, :, t] = rows[:, t * 128:(t + 1) * 128].reshape(CHIPS, 8, 128).astype(BF16)

    def exchange(l):
        def go(k, _):
            pb, pxl = shift_at(b, xl, 64 - k)
            pltpu.make_async_remote_copy(
                src_ref=send1.at[l, pb * 2 + pxl],
                dst_ref=recv1[l].at[xl, pl.ds(b * 4, 4)],
                send_sem=s1.at[l], recv_sem=r1.at[l],
                device_id=device(pb, pxl), device_id_type=MESH,
            ).start()
            return 0

        lax.fori_loop(1, CHIPS, go, 0)
        pltpu.make_async_copy(send1.at[l, chip], recv1[l].at[xl, pl.ds(b * 4, 4)], r1.at[l]).start()

    permute(0)
    pl.semaphore_wait(bar, 65)
    exchange(0)
    permute(1)
    exchange(1)
    permute(2)
    exchange(2)

    lane8, row8 = iota((8, 128), 1), iota((8, 128), 0)
    first = jnp.where(lane8 == row8, 1.0, 0.0).astype(BF16)
    last = jnp.where(lane8 == row8 + 120, 1.0, 0.0).astype(BF16)
    nt = (((1,), (1,)), ((), ()))
    for l in range(LAYERS):
        halo_s[0, l] = lax.dot_general(
            last, x[l, :, BLK - 128:], nt, preferred_element_type=F32).astype(BF16)
        halo_s[1, l] = lax.dot_general(
            first, x[l, :, :128], nt, preferred_element_type=F32).astype(BF16)
    halos = [
        pltpu.make_async_remote_copy(
            src_ref=halo_s.at[i], dst_ref=halo_r.at[i], send_sem=hs.at[i], recv_sem=hr.at[i],
            device_id=dev, device_id_type=MESH)
        for i, dev in enumerate((right, left))
    ]
    for h in halos:
        h.start()

    px0 = (iota((16, 128), 0) * 128).astype(F32)
    px = px0 + iota((16, 128), 1).astype(F32)
    for d in range(DIRS):
        for l in range(LAYERS):
            num = ratio[l, 0, d].astype(F32)
            den = ratio[l, 1, d].astype(F32)
            start = (offs[l, 1, d] - wind[1, l] + COLS) & (COLS - 1)
            a = px * num
            qv = floor_div(a, den)
            tile = (start + floor_div(px0 * num, den).astype(I32)) >> 7
            relb[d * LAYERS + l] = start + qv.astype(I32) - tile * 128
            frac[d * LAYERS + l] = (a - qv * den) / den

    pupil = (b * NPR + iota((NPR, 1), 0)).astype(F32)

    def row_weights(l, mrow):
        num = ratio[l, 0, q].astype(F32)
        den = ratio[l, 1, q].astype(F32)
        start = (offs[l, 0, q] - wind[0, l] + ROWS) & (ROWS - 1)
        a = pupil * num
        qv = floor_div(a, den)
        f = (a - qv * den) / den
        base = (start + qv.astype(I32)) & 63
        high = f.astype(BF16).astype(F32)
        low = (1.0 - f).astype(BF16).astype(F32)
        return jnp.where(mrow == base, low, 0.0) + jnp.where(mrow == ((base + 1) & 63), high, 0.0)

    ca = iota((NPR, CHIPS * 24), 1)
    ma = (ca * 2731) >> 16
    ja = ca - ma * 24
    wa = jnp.where(ja < 10, row_weights(0, ma), row_weights(1, ma))
    for j in range(JT):
        wbig_a[j * NPR:(j + 1) * NPR] = jnp.where((ja == j) | (ja == j + 10), wa, 0.0).astype(BF16)
    cb = iota((NPR, CHIPS * 16), 1)
    wb = row_weights(2, cb >> 4)
    for j in range(JT):
        wbig_b[j * NPR:(j + 1) * NPR] = jnp.where((cb & 15) == j, wb, 0.0).astype(BF16)

    for load in tables:
        load.wait()
    g32 = jnp.where((iota((32, 32), 0) >> 4) == (iota((32, 32), 1) >> 4), 1.0, 0.0)
    g128 = jnp.where((iota((128, 128), 0) >> 4) == (iota((128, 128), 1) >> 4), 1.0, 0.0)
    for j in range(JT):
        av = amp[:, j * 128:(j + 1) * 128]
        energy = jnp.dot(g32, av * av, precision=HIGHEST, preferred_element_type=F32)
        energy = jnp.dot(energy, g128, precision=HIGHEST, preferred_element_type=F32)
        ampn[j] = av / jnp.sqrt(energy)

    for h in halos:
        h.wait()
    tn = (((0,), (0,)), ((), ()))
    lane = iota((BLK, 128), 1)
    for l in range(LAYERS):
        w1 = wind[1, l]
        lanes = [lax.dot_general(halo_r[0, l], last, tn, preferred_element_type=F32)]
        lanes += [x[l, :, t * 128:(t + 1) * 128].astype(F32) for t in range(4)]
        lanes += [lax.dot_general(halo_r[1, l], first, tn, preferred_element_type=F32)]
        turned = [pltpu.roll(v, (w1 + 128) & 127, 1) for v in lanes]
        before, after = lane < w1, lane >= 128 + w1
        for t in range(4):
            val = jnp.where(before, turned[t], jnp.where(after, turned[t + 2], turned[t + 1]))
            y[l, 8:8 + BLK, t * 128:(t + 1) * 128] = val
        edge_s[0, l] = y[l, BLK:BLK + 8].astype(BF16)
        edge_s[1, l] = y[l, 8:16].astype(BF16)
    edges = [
        pltpu.make_async_remote_copy(
            src_ref=edge_s.at[i], dst_ref=edge_r.at[i], send_sem=es.at[i], recv_sem=er.at[i],
            device_id=dev, device_id_type=MESH)
        for i, dev in enumerate((up, down))
    ]
    for e in edges:
        e.start()

    def flow_rows():
        for e in edges:
            e.wait()
        for l in range(LAYERS):
            y[l, 0:8] = edge_r[0, l].astype(F32)
            y[l, BLK + 8:BLK + 16] = edge_r[1, l].astype(F32)
            w0 = wind[0, l]
            turn, whole = w0 & 7, w0 >> 3
            keep = iota((BLK // 8 + 1, 8, 128), 1) >= turn
            for t in range(4):
                part = y[l, :, t * 128:(t + 1) * 128].reshape(BLK // 8 + 2, 8, 128)
                part = pltpu.roll(part, turn, 1)
                part = jnp.concatenate([part[:1], jnp.where(keep, part[1:], part[:-1])], axis=0)
                val = jnp.where(whole > 0, part[:-2], jnp.where(whole == 0, part[1:-1], part[2:]))
                x[l, :, t * 128:(t + 1) * 128] = val.reshape(BLK, 128).astype(BF16)
            pltpu.make_async_copy(x.at[l], new_out.at[l], osem.at[l]).start()

    def columns(l):
        def one(i, _):
            d, j = i // JT, i % JT
            num, den = ratio[l, 0, d], ratio[l, 1, d]
            start = (offs[l, 1, d] - wind[1, l] + COLS) & (COLS - 1)
            tile = (start + stretch(j, 128, num, den, magic[den])) >> 7
            rel = relb[d * LAYERS + l, pl.ds(j, 1), :]
            f = frac[d * LAYERS + l, pl.ds(j, 1), :]
            high = f.astype(BF16).astype(F32)
            low = (1.0 - f).astype(BF16).astype(F32)
            rel = jnp.broadcast_to(rel, (8, 128))
            rel_u = rel + 1
            idx, idx_u = rel & 127, rel_u & 127
            sel, sel_u = rel >> 7, rel_u >> 7
            for h in range(2):
                t = [recv1[l][h, (tile + s) & 127].astype(F32) for s in range(3)]
                g = [jnp.take_along_axis(v, idx, axis=1) for v in t]
                u = [jnp.take_along_axis(v, idx_u, axis=1) for v in t]
                vb = jnp.where(sel == 0, g[0], jnp.where(sel == 1, g[1], g[2]))
                vu = jnp.where(sel_u == 0, u[0], jnp.where(sel_u == 1, u[1], u[2]))
                out = low * vb + high * vu
                cols[l].at[d % 2, c, d // 2, h].reshape(128, 128)[pl.ds(j, 8, stride=16), :] = out
            return 0

        lax.fori_loop(0, DIRS * JT, one, 0)

    def swap(l):
        return pltpu.make_async_remote_copy(
            src_ref=cols[l].at[1 - c, c], dst_ref=cols[l].at[1 - c, c],
            send_sem=ws.at[l], recv_sem=wr.at[l],
            device_id=(b, xl * 2 + 1 - c), device_id_type=MESH)

    def arrive(l):
        pltpu.make_async_copy(recv1[l], recv1[l], r1.at[l]).wait()
        columns(l)
        swap(l).start()

    def row_of(l, p, pxl):
        d = pxl * 2 + c
        num, den = ratio[l, 0, d], ratio[l, 1, d]
        s = offs[l, 0, d] - wind[0, l] + ROWS + stretch(p, NPR, num, den, magic[den])
        k = ((s + ((chip - s) & 63)) & (ROWS - 1)) >> 6
        val = cols[l][c, (k >> 3) & 1, pxl, k >> 4, k & 7]
        return val[:8], val[8:]

    sub = iota((8, 128), 0)

    def deliver(src, dst, i, k, pb, pxl):
        @pl.when(k > 0)
        def _():
            pltpu.make_async_remote_copy(
                src_ref=src.at[pb * 2 + pxl], dst_ref=dst.at[chip],
                send_sem=s2.at[i], recv_sem=r2.at[i],
                device_id=device(pb, pxl), device_id_type=MESH,
            ).start()

        @pl.when(k == 0)
        def _():
            pltpu.make_async_copy(src.at[chip], dst.at[chip], r2.at[i]).start()

    def send_a(i, _):
        k = 63 - i
        pb, pxl = shift_at(b, xl, k)
        a0, a1 = row_of(0, pb, pxl)
        b0, b1 = row_of(1, pb, pxl)
        b0, b1 = pltpu.roll(b0, 2, 0), pltpu.roll(b1, 2, 0)
        send2a[pb * 2 + pxl, 0] = a0.astype(BF16)
        send2a[pb * 2 + pxl, 1] = jnp.where(sub < 2, a1, b0).astype(BF16)
        send2a[pb * 2 + pxl, 2] = jnp.where(sub < 2, b0, jnp.where(sub < 4, b1, 0.0)).astype(BF16)
        deliver(send2a, recv2a, 0, k, pb, pxl)
        return 0

    def send_b(i, _):
        k = 63 - i
        pb, pxl = shift_at(b, xl, k)
        a0, a1 = row_of(2, pb, pxl)
        send2b[pb * 2 + pxl, 0] = a0.astype(BF16)
        send2b[pb * 2 + pxl, 1] = jnp.where(sub < 2, a1, 0.0).astype(BF16)
        deliver(send2b, recv2b, 1, k, pb, pxl)
        return 0

    arrive(0)
    flow_rows()
    arrive(1)
    swap(0).wait()
    swap(1).wait()
    lax.fori_loop(0, CHIPS, send_a, 0)
    arrive(2)
    swap(2).wait()
    lax.fori_loop(0, CHIPS, send_b, 0)

    pltpu.make_async_copy(recv2a, recv2a, r2.at[0]).wait()
    phase[...] = jnp.dot(
        wbig_a[...], recv2a[...].reshape(CHIPS * 24, 128), preferred_element_type=F32)
    pltpu.make_async_copy(recv2b, recv2b, r2.at[1]).wait()
    phase[...] += jnp.dot(
        wbig_b[...], recv2b[...].reshape(CHIPS * 16, 128), preferred_element_type=F32)
    for j in range(JT):
        sin, cos = sincos(phase[j * NPR:(j + 1) * NPR])
        field[0, j] = ampn[j] * cos
        field[1, j] = ampn[j] * sin
    for j in range(JT):
        both = jnp.concatenate([field[0, j], field[1, j]], axis=0)
        g = jnp.dot(both, dcol[...], precision=HIGHEST, preferred_element_type=F32)
        half_re = g[:32, :256] - g[32:, 256:]
        half_im = g[:32, 256:] + g[32:, :256]
        half = jnp.concatenate([half_re, half_im], axis=0)
        full = jnp.dot(drow[...], half, precision=HIGHEST, preferred_element_type=F32)
        spots[:, j * 256:(j + 1) * 256] = full[:64] * full[:64] + full[64:] * full[64:]

    for l in range(LAYERS):
        pltpu.make_async_copy(send1.at[l, 0:63], send1.at[l, 0:63], s1.at[l]).wait()
        pltpu.make_async_copy(x.at[l], new_out.at[l], osem.at[l]).wait()
    pltpu.make_async_copy(send2a.at[0:63], send2a.at[0:63], s2.at[0]).wait()
    pltpu.make_async_copy(send2b.at[0:63], send2b.at[0:63], s2.at[1]).wait()


def per_device(screens, amplitude, wind, offsets, ratio):
    cols, rows = dft_tables()
    vmem = pl.BlockSpec(memory_space=pltpu.VMEM)
    smem = pl.BlockSpec(memory_space=pltpu.SMEM)
    hbm = pl.BlockSpec(memory_space=pl.ANY)
    dma = pltpu.SemaphoreType.DMA
    new, spots = pl.pallas_call(
        kernel,
        out_shape=(
            jax.ShapeDtypeStruct((LAYERS, BLK, BLK), BF16),
            jax.ShapeDtypeStruct((64, 2560), F32),
        ),
        in_specs=[smem, smem, smem, smem, hbm, hbm, hbm, hbm],
        out_specs=(hbm, vmem),
        scratch_shapes=[
            pltpu.VMEM((LAYERS, BLK, BLK), BF16),
            pltpu.VMEM((NPR, PC), F32),
            pltpu.VMEM((128, 512), F32),
            pltpu.VMEM((128, 64), F32),
            pltpu.VMEM((LAYERS, CHIPS, 4, 8, 128), BF16),
            pltpu.VMEM((2, 128, 8, 128), BF16),
            pltpu.VMEM((2, 128, 8, 128), BF16),
            pltpu.VMEM((2, 128, 8, 128), BF16),
            pltpu.VMEM((2, LAYERS, 8, BLK), BF16),
            pltpu.VMEM((2, LAYERS, 8, BLK), BF16),
            pltpu.VMEM((2, LAYERS, 8, BLK), BF16),
            pltpu.VMEM((2, LAYERS, 8, BLK), BF16),
            pltpu.VMEM((LAYERS, BLK + 16, BLK), F32),
            pltpu.VMEM((DIRS * LAYERS, 16, 128), I32),
            pltpu.VMEM((DIRS * LAYERS, 16, 128), F32),
            pltpu.VMEM((2, 2, 2, 2, 8, 16, 128), F32),
            pltpu.VMEM((2, 2, 2, 2, 8, 16, 128), F32),
            pltpu.VMEM((2, 2, 2, 2, 8, 16, 128), F32),
            pltpu.VMEM((CHIPS, 3, 8, 128), BF16),
            pltpu.VMEM((CHIPS, 2, 8, 128), BF16),
            pltpu.VMEM((CHIPS, 3, 8, 128), BF16),
            pltpu.VMEM((CHIPS, 2, 8, 128), BF16),
            pltpu.VMEM((JT * NPR, CHIPS * 24), BF16),
            pltpu.VMEM((JT * NPR, CHIPS * 16), BF16),
            pltpu.VMEM((JT, NPR, 128), F32),
            pltpu.VMEM((JT * NPR, 128), F32),
            pltpu.VMEM((2, JT, NPR, 128), F32),
            dma((3,)), dma((3,)), dma((3,)), dma((3,)), dma((2,)), dma((2,)), dma((2,)), dma((2,)),
            dma((3,)), dma((3,)), dma((2,)), dma((2,)), dma((3,)),
        ],
        compiler_params=pltpu.CompilerParams(
            collective_id=0, has_side_effects=True, vmem_limit_bytes=63 << 20),
        name="screens_to_spots",
    )(wind.T, offsets.transpose(1, 2, 0), ratio.transpose(1, 2, 0), jnp.asarray(reciprocals()), screens, amplitude, jnp.asarray(cols), jnp.asarray(rows))
    return new, spots[None]


def solution(mesh):
    return jax.shard_map(
        per_device,
        mesh=mesh,
        in_specs=(P(None, "dir", "layer"), P("layer", None), P(), P(), P()),
        out_specs=(P(None, "dir", "layer"), P("dir", "layer", None)),
        check_vma=False,
    )
```

```python
import jax
import jax.numpy as jnp
import numpy as np
from jax import lax
from jax.experimental import pallas as pl
from jax.experimental.pallas import tpu as pltpu
from jax.sharding import PartitionSpec as P

MESH = pl.DeviceIdType.MESH
SUB = 16
SPOT = 32
HALO = 8
LAYERS = 3
DIRS = 4
ROWS, COLS = 2048, 16384
PR, PC = 1024, 1280
BLK = 512
CHIPS = 64
JT = PC // 128
NPR = 32
F32, BF16, I32 = jnp.float32, jnp.bfloat16, jnp.int32
HIGHEST = lax.Precision.HIGHEST


def iota(shape, dim):
    return lax.broadcasted_iota(I32, shape, dim)


def floor_div(a, den):
    q = jnp.floor(a / den)
    r = a - q * den
    q = q + jnp.where(r >= den, 1.0, 0.0) - jnp.where(r < 0.0, 1.0, 0.0)
    return q


def reciprocals():
    den = np.maximum(np.arange(129), 1)
    return (2 ** 21 // den + 1).astype(np.int32)


def stretch(i, unit, num, den, mul):
    part = i * (num - den)
    whole = (part * mul) >> 21
    rest = part - whole * den
    return unit * (i + whole) + ((unit * rest * mul) >> 21)


def sincos(x):
    n = jnp.floor(x * np.float32(2.0 / np.pi) + 0.5)
    r = x - n * np.float32(1.5703125)
    r = r - n * np.float32(4.837512969970703125e-4)
    r = r - n * np.float32(7.54978995489188216e-8)
    r2 = r * r
    s = r + r * r2 * (
        np.float32(-1.6666654611e-1)
        + r2 * (np.float32(8.3321608736e-3) + r2 * np.float32(-1.9515295891e-4))
    )
    c = (
        1.0
        - 0.5 * r2
        + r2 * r2 * (
            np.float32(4.166664568298827e-2)
            + r2 * (np.float32(-1.388731625493765e-3) + r2 * np.float32(2.443315711809948e-5))
        )
    )
    k = n.astype(I32)
    swap = (k & 1) == 1
    sin = jnp.where(swap, c, s)
    cos = jnp.where(swap, s, c)
    sin = jnp.where((k & 2) == 2, -sin, sin)
    cos = jnp.where(((k + 1) & 2) == 2, -cos, cos)
    return sin, cos


def dft_tables():
    turns = ((np.arange(SPOT)[:, None] - SPOT // 2) * np.arange(SUB)[None, :]) % SPOT
    angle = turns * (2.0 * np.pi / SPOT)
    c, s = np.cos(angle), -np.sin(angle)
    cols = np.concatenate([np.kron(np.eye(8), c.T), np.kron(np.eye(8), s.T)], axis=1)
    cb, sb = np.kron(np.eye(2), c), np.kron(np.eye(2), s)
    rows = np.block([[cb, -sb], [sb, cb]])
    return cols.astype(np.float32), rows.astype(np.float32)


def shift_at(b, xl, k):
    px = ((b >> 4) * 2 + xl + (k & 3)) & 3
    py = ((b >> 2) + (k >> 2)) & 3
    pz = (b + (k >> 4)) & 3
    return (px >> 1) * 16 + py * 4 + pz, px & 1


def kernel(
    wind, offs, ratio, magic, screens, amp_h, dcol_h, drow_h,
    new_out, spots,
    x, amp, dcol, drow, send1, recv_a, recv_b, recv_c, side_s, side_r, edge_s, edge_r, y,
    relb, frac, cols, mate_a, mate_b, mate_c, rows_a, rows_b, rows_c, kidx,
    send2a, send2b, recv2a, recv2b, wbig_a, wbig_b, ampn, phase, field,
    in_sem, tab_sem, s1, r1, hs, hr, ws, wr, s2, r2, osem,
):
    recv1 = (recv_a, recv_b, recv_c)
    mate, rows = (mate_a, mate_b, mate_c), (rows_a, rows_b, rows_c)
    b = lax.axis_index("layer")
    q = lax.axis_index("dir")
    xl, c = q // 2, q % 2
    chip = b * 2 + xl

    def device(pb, pxl):
        return (pb, pxl * 2 + c)

    def block(db, dq):
        return ((b + db) & 31, (q + dq) & 3)

    near = [(db, dq) for db in (-1, 0, 1) for dq in (-1, 1)]
    bar = pltpu.get_barrier_semaphore()
    for n in near:
        pl.semaphore_signal(bar, inc=1, device_id=block(*n), device_id_type=MESH)

    def greet(k, _):
        pl.semaphore_signal(bar, inc=1, device_id=device(*shift_at(b, xl, 64 - k)), device_id_type=MESH)
        return 0

    lax.fori_loop(1, CHIPS, greet, 0)

    loads = [pltpu.make_async_copy(screens.at[l], x.at[l], in_sem.at[l]) for l in range(LAYERS)]
    tables = [
        pltpu.make_async_copy(src, dst, tab_sem.at[i])
        for i, (src, dst) in enumerate(((amp_h, amp), (dcol_h, dcol), (drow_h, drow)))
    ]
    for load in loads + tables:
        load.start()

    ro, ri = iota((BLK, BLK), 0), iota((BLK, BLK), 1)
    perm = jnp.where(ri == (ro & 7) * 64 + (ro >> 3), 1.0, 0.0).astype(BF16)

    def permute(l):
        loads[l].wait()
        ordered = jnp.dot(perm, x[l], preferred_element_type=F32)
        for t in range(4):
            send1[l, :, t] = ordered[:, t * 128:(t + 1) * 128].reshape(CHIPS, 8, 128).astype(BF16)

    def exchange(l):
        def go(k, _):
            pb, pxl = shift_at(b, xl, 64 - k)
            pltpu.make_async_remote_copy(
                src_ref=send1.at[l, pb * 2 + pxl],
                dst_ref=recv1[l].at[xl, pl.ds(b * 4, 4)],
                send_sem=s1.at[l], recv_sem=r1.at[l],
                device_id=device(pb, pxl), device_id_type=MESH,
            ).start()
            return 0

        lax.fori_loop(1, CHIPS, go, 0)
        pltpu.make_async_copy(send1.at[l, chip], recv1[l].at[xl, pl.ds(b * 4, 4)], r1.at[l]).start()

    def sent(l):
        pltpu.make_async_copy(send1.at[l, 0:63], send1.at[l, 0:63], s1.at[l]).wait()

    permute(0)
    pl.semaphore_wait(bar, 63 + len(near))
    exchange(0)
    permute(1)
    permute(2)

    lane8, row8 = iota((8, 128), 1), iota((8, 128), 0)
    first = jnp.where(lane8 == row8, 1.0, 0.0).astype(BF16)
    last = jnp.where(lane8 == row8 + 120, 1.0, 0.0).astype(BF16)
    nt = (((1,), (1,)), ((), ()))
    for l in range(LAYERS):
        side_s[0, l] = lax.dot_general(
            last, x[l, :, BLK - 128:], nt, preferred_element_type=F32).astype(BF16)
        side_s[1, l] = lax.dot_general(
            first, x[l, :, :128], nt, preferred_element_type=F32).astype(BF16)
        edge_s[0, l] = x[l, BLK - 8:]
        edge_s[1, l] = x[l, :8]

    def halo(i, src, dst, to):
        return pltpu.make_async_remote_copy(
            src_ref=src, dst_ref=dst, send_sem=hs.at[i], recv_sem=hr.at[i],
            device_id=to, device_id_type=MESH)

    halos = []
    for i, db in enumerate((1, -1)):
        dst = side_r.at[i]
        halos.append(halo(4 * i, side_s.at[i], dst.at[:, :, 128:128 + BLK], block(db, 0)))
        halos.append(halo(4 * i + 1, side_s.at[i, :, :, BLK - 128:], dst.at[:, :, :128], block(db, 1)))
        halos.append(halo(4 * i + 2, side_s.at[i, :, :, :128], dst.at[:, :, 128 + BLK:], block(db, -1)))
        halos.append(halo(4 * i + 3, edge_s.at[i], edge_r.at[i], block(0, db)))
    for h in halos:
        h.start()

    sent(0)
    exchange(1)

    def row_table(p, _):
        for l in range(LAYERS):
            for pxl in range(2):
                d = pxl * 2 + c
                num, den = ratio[l, 0, d], ratio[l, 1, d]
                r = offs[l, 0, d] - wind[0, l] + ROWS + stretch(p, NPR, num, den, magic[den])
                kidx[l, p * 2 + pxl] = ((r + ((chip - r) & 63)) & (ROWS - 1)) >> 6
        return 0

    lax.fori_loop(0, 32, row_table, 0)
    cols[...] = jnp.zeros_like(cols)

    px0 = (iota((16, 128), 0) * 128).astype(F32)
    px = px0 + iota((16, 128), 1).astype(F32)
    for d in range(DIRS):
        for l in range(LAYERS):
            num = ratio[l, 0, d].astype(F32)
            den = ratio[l, 1, d].astype(F32)
            start = (offs[l, 1, d] - wind[1, l] + COLS) & (COLS - 1)
            a = px * num
            qv = floor_div(a, den)
            tile = (start + floor_div(px0 * num, den).astype(I32)) >> 7
            relb[d * LAYERS + l] = start + qv.astype(I32) - tile * 128
            frac[d * LAYERS + l] = (a - qv * den) / den

    pupil = (b * NPR + iota((NPR, 1), 0)).astype(F32)

    def row_weights(l, mrow):
        num = ratio[l, 0, q].astype(F32)
        den = ratio[l, 1, q].astype(F32)
        start = (offs[l, 0, q] - wind[0, l] + ROWS) & (ROWS - 1)
        a = pupil * num
        qv = floor_div(a, den)
        f = (a - qv * den) / den
        base = (start + qv.astype(I32)) & 63
        high = f.astype(BF16).astype(F32)
        low = (1.0 - f).astype(BF16).astype(F32)
        return jnp.where(mrow == base, low, 0.0) + jnp.where(mrow == ((base + 1) & 63), high, 0.0)

    ca = iota((NPR, CHIPS * 24), 1)
    ma = (ca * 2731) >> 16
    ja = ca - ma * 24
    wa = jnp.where(ja < 10, row_weights(0, ma), row_weights(1, ma))
    for j in range(JT):
        wbig_a[j * NPR:(j + 1) * NPR] = jnp.where((ja == j) | (ja == j + 10), wa, 0.0).astype(BF16)
    cb = iota((NPR, CHIPS * 16), 1)
    wb = row_weights(2, cb >> 4)
    for j in range(JT):
        wbig_b[j * NPR:(j + 1) * NPR] = jnp.where((cb & 15) == j, wb, 0.0).astype(BF16)

    for load in tables:
        load.wait()
    g32 = jnp.where((iota((32, 32), 0) >> 4) == (iota((32, 32), 1) >> 4), 1.0, 0.0)
    g128 = jnp.where((iota((128, 128), 0) >> 4) == (iota((128, 128), 1) >> 4), 1.0, 0.0)
    for j in range(JT):
        av = amp[:, j * 128:(j + 1) * 128]
        energy = jnp.dot(g32, av * av, precision=HIGHEST, preferred_element_type=F32)
        energy = jnp.dot(energy, g128, precision=HIGHEST, preferred_element_type=F32)
        ampn[j] = av / jnp.sqrt(energy)

    sent(1)
    exchange(2)
    for h in halos:
        h.wait()
    tn = (((0,), (0,)), ((), ()))
    for l in range(LAYERS):
        w0, w1 = wind[0, l], wind[1, l]
        left = lax.dot_general(side_r[0, l], last, tn, preferred_element_type=F32)
        right = lax.dot_general(side_r[1, l], first, tn, preferred_element_type=F32)
        for r0, n, src in ((0, 8, edge_r.at[0, l]), (8, BLK, x.at[l]), (BLK + 8, 8, edge_r.at[1, l])):
            at = r0 + 120
            lanes = [left[at:at + n]]
            lanes += [src[:, t * 128:(t + 1) * 128].astype(F32) for t in range(4)]
            lanes += [right[at:at + n]]
            turned = [pltpu.roll(v, (w1 + 128) & 127, 1) for v in lanes]
            lane = iota((n, 128), 1)
            before, after = lane < w1, lane >= 128 + w1
            for t in range(4):
                y[r0:r0 + n, t * 128:(t + 1) * 128] = jnp.where(
                    before, turned[t], jnp.where(after, turned[t + 2], turned[t + 1]))
        turn, whole = w0 & 7, w0 >> 3
        keep = iota((BLK // 8 + 1, 8, 128), 1) >= turn
        for t in range(4):
            part = y[:, t * 128:(t + 1) * 128].reshape(BLK // 8 + 2, 8, 128)
            part = pltpu.roll(part, turn, 1)
            part = jnp.concatenate([part[:1], jnp.where(keep, part[1:], part[:-1])], axis=0)
            val = jnp.where(whole > 0, part[:-2], jnp.where(whole == 0, part[1:-1], part[2:]))
            x[l, :, t * 128:(t + 1) * 128] = val.reshape(BLK, 128).astype(BF16)
        pltpu.make_async_copy(x.at[l], new_out.at[l], osem.at[l]).start()

    def columns(l):
        def one(d, j):
            num, den = ratio[l, 0, d], ratio[l, 1, d]
            start = (offs[l, 1, d] - wind[1, l] + COLS) & (COLS - 1)
            tile = (start + stretch(j, 128, num, den, magic[den])) >> 7
            rel = relb[d * LAYERS + l, pl.ds(j, 1), :]
            f = frac[d * LAYERS + l, pl.ds(j, 1), :]
            high = f.astype(BF16).astype(F32)
            low = (1.0 - f).astype(BF16).astype(F32)
            rel = jnp.broadcast_to(rel, (8, 128))
            rel_u = rel + 1
            idx, idx_u = rel & 127, rel_u & 127
            sel, sel_u = rel >> 7, rel_u >> 7
            for h in range(2):
                t = [recv1[l][h, (tile + s) & 127].astype(F32) for s in range(3)]
                g = [jnp.take_along_axis(v, idx, axis=1) for v in t]
                u = [jnp.take_along_axis(v, idx_u, axis=1) for v in t]
                vb = jnp.where(sel == 0, g[0], jnp.where(sel == 1, g[1], g[2]))
                vu = jnp.where(sel_u == 0, u[0], jnp.where(sel_u == 1, u[1], u[2]))
                out = low * vb + high * vu
                cols.at[d % 2, d // 2, h].reshape(128, 128)[pl.ds(j, 8, stride=16), :] = out

        def direction(d, _):
            for j in range(JT):
                one(d, j)
            return 0

        lax.fori_loop(0, DIRS, direction, 0)
        mate[l][...] = cols[1 - c].astype(BF16)
        rows[l][c] = cols[c].astype(BF16)

    def swap(l):
        return pltpu.make_async_remote_copy(
            src_ref=mate[l], dst_ref=rows[l].at[c],
            send_sem=ws.at[l], recv_sem=wr.at[l],
            device_id=(b, xl * 2 + 1 - c), device_id_type=MESH)

    def arrive(l):
        pltpu.make_async_copy(recv1[l], recv1[l], r1.at[l]).wait()
        columns(l)
        swap(l).start()

    def row_of(l, dest):
        k = kidx[l, dest]
        return rows[l][(k >> 3) & 1, dest & 1, k >> 4, k & 7]

    sub = iota((8, 128), 0)

    def pack_a(dest):
        val_a, val_b = row_of(0, dest).astype(F32), row_of(1, dest).astype(F32)
        b0, b1 = pltpu.roll(val_b[:8], 2, 0), pltpu.roll(val_b[8:], 2, 0)
        send2a[dest, 0] = val_a[:8].astype(BF16)
        send2a[dest, 1] = jnp.where(sub < 2, val_a[8:], b0).astype(BF16)
        send2a[dest, 2] = jnp.where(sub < 2, b0, b1).astype(BF16)

    def pack_b(dest):
        send2b[dest] = row_of(2, dest)

    def deliver(i, src, dst, pack):
        def some(n, _):
            for u in range(7):
                pb, pxl = shift_at(b, xl, 63 - n * 7 - u)
                pack(pb * 2 + pxl)
            for u in range(7):
                pb, pxl = shift_at(b, xl, 63 - n * 7 - u)
                pltpu.make_async_remote_copy(
                    src_ref=src.at[pb * 2 + pxl], dst_ref=dst.at[chip],
                    send_sem=s2.at[i], recv_sem=r2.at[i],
                    device_id=device(pb, pxl), device_id_type=MESH,
                ).start()
            return 0

        lax.fori_loop(0, 9, some, 0)
        pack(chip)
        pltpu.make_async_copy(src.at[chip], dst.at[chip], r2.at[i]).start()

    arrive(0)
    arrive(1)
    swap(0).wait()
    swap(1).wait()
    deliver(0, send2a, recv2a, pack_a)
    arrive(2)
    swap(2).wait()
    deliver(1, send2b, recv2b, pack_b)

    pltpu.make_async_copy(recv2a, recv2a, r2.at[0]).wait()
    phase[...] = jnp.dot(
        wbig_a[...], recv2a[...].reshape(CHIPS * 24, 128), preferred_element_type=F32)
    pltpu.make_async_copy(recv2b, recv2b, r2.at[1]).wait()
    phase[...] += jnp.dot(
        wbig_b[...], recv2b[...].reshape(CHIPS * 16, 128), preferred_element_type=F32)
    for j in range(JT):
        sin, cos = sincos(phase[j * NPR:(j + 1) * NPR])
        field[0, j] = ampn[j] * cos
        field[1, j] = ampn[j] * sin
    for j in range(JT):
        both = jnp.concatenate([field[0, j], field[1, j]], axis=0)
        g = jnp.dot(both, dcol[...], precision=HIGHEST, preferred_element_type=F32)
        half_re = g[:32, :256] - g[32:, 256:]
        half_im = g[:32, 256:] + g[32:, :256]
        half = jnp.concatenate([half_re, half_im], axis=0)
        full = jnp.dot(drow[...], half, precision=HIGHEST, preferred_element_type=F32)
        spots[:, j * 256:(j + 1) * 256] = full[:64] * full[:64] + full[64:] * full[64:]

    for l in range(LAYERS):
        pltpu.make_async_copy(x.at[l], new_out.at[l], osem.at[l]).wait()
    sent(2)
    pltpu.make_async_copy(send2a.at[0:63], send2a.at[0:63], s2.at[0]).wait()
    pltpu.make_async_copy(send2b.at[0:63], send2b.at[0:63], s2.at[1]).wait()


def per_device(screens, amplitude, wind, offsets, ratio):
    cols, rows = dft_tables()
    vmem = pl.BlockSpec(memory_space=pltpu.VMEM)
    smem = pl.BlockSpec(memory_space=pltpu.SMEM)
    hbm = pl.BlockSpec(memory_space=pl.ANY)
    dma = pltpu.SemaphoreType.DMA
    new, spots = pl.pallas_call(
        kernel,
        out_shape=(
            jax.ShapeDtypeStruct((LAYERS, BLK, BLK), BF16),
            jax.ShapeDtypeStruct((64, 2560), F32),
        ),
        in_specs=[smem, smem, smem, smem, hbm, hbm, hbm, hbm],
        out_specs=(hbm, vmem),
        scratch_shapes=[
            pltpu.VMEM((LAYERS, BLK, BLK), BF16),
            pltpu.VMEM((NPR, PC), F32),
            pltpu.VMEM((128, 512), F32),
            pltpu.VMEM((128, 64), F32),
            pltpu.VMEM((LAYERS, CHIPS, 4, 8, 128), BF16),
            pltpu.VMEM((2, 128, 8, 128), BF16),
            pltpu.VMEM((2, 128, 8, 128), BF16),
            pltpu.VMEM((2, 128, 8, 128), BF16),
            pltpu.VMEM((2, LAYERS, 8, BLK), BF16),
            pltpu.VMEM((2, LAYERS, 8, BLK + 256), BF16),
            pltpu.VMEM((2, LAYERS, 8, BLK), BF16),
            pltpu.VMEM((2, LAYERS, 8, BLK), BF16),
            pltpu.VMEM((BLK + 16, BLK), F32),
            pltpu.VMEM((DIRS * LAYERS, 16, 128), I32),
            pltpu.VMEM((DIRS * LAYERS, 16, 128), F32),
            pltpu.VMEM((2, 2, 2, 8, 16, 128), F32),
            *[pltpu.VMEM((2, 2, 8, 16, 128), BF16)] * 3,
            *[pltpu.VMEM((2, 2, 2, 8, 16, 128), BF16)] * 3,
            pltpu.SMEM((LAYERS, CHIPS), I32),
            pltpu.VMEM((CHIPS, 3, 8, 128), BF16),
            pltpu.VMEM((CHIPS, 16, 128), BF16),
            pltpu.VMEM((CHIPS, 3, 8, 128), BF16),
            pltpu.VMEM((CHIPS, 16, 128), BF16),
            pltpu.VMEM((JT * NPR, CHIPS * 24), BF16),
            pltpu.VMEM((JT * NPR, CHIPS * 16), BF16),
            pltpu.VMEM((JT, NPR, 128), F32),
            pltpu.VMEM((JT * NPR, 128), F32),
            pltpu.VMEM((2, JT, NPR, 128), F32),
            dma((3,)), dma((3,)), dma((3,)), dma((3,)), dma((8,)), dma((8,)),
            dma((3,)), dma((3,)), dma((2,)), dma((2,)), dma((3,)),
        ],
        compiler_params=pltpu.CompilerParams(
            collective_id=0, has_side_effects=True, vmem_limit_bytes=63 << 20),
        name="screens_to_spots",
    )(wind.T, offsets.transpose(1, 2, 0), ratio.transpose(1, 2, 0), jnp.asarray(reciprocals()), screens, amplitude, jnp.asarray(cols), jnp.asarray(rows))
    return new, spots[None]


def solution(mesh):
    return jax.shard_map(
        per_device,
        mesh=mesh,
        in_specs=(P(None, "dir", "layer"), P("layer", None), P(), P(), P()),
        out_specs=(P(None, "dir", "layer"), P("dir", "layer", None)),
        check_vma=False,
    )
```

```python
import jax
import jax.numpy as jnp
import ml_dtypes
import numpy as np
from jax import lax
from jax.experimental import pallas as pl
from jax.experimental.pallas import tpu as pltpu
from jax.sharding import PartitionSpec as P

MESH = pl.DeviceIdType.MESH
SUB = 16
SPOT = 32
HALO = 8
LAYERS = 3
DIRS = 4
ROWS, COLS = 2048, 16384
PR, PC = 1024, 1280
BLK = 512
CHIPS = 64
JT = PC // 128
NPR = 32
F32, BF16, I32 = jnp.float32, jnp.bfloat16, jnp.int32
HIGHEST = lax.Precision.HIGHEST


def iota(shape, dim):
    return lax.broadcasted_iota(I32, shape, dim)


def floor_div(a, den):
    q = jnp.floor(a / den)
    r = a - q * den
    q = q + jnp.where(r >= den, 1.0, 0.0) - jnp.where(r < 0.0, 1.0, 0.0)
    return q


def reciprocals():
    den = np.maximum(np.arange(129), 1)
    return (2 ** 21 // den + 1).astype(np.int32)


def stretch(i, unit, num, den, mul):
    part = i * (num - den)
    whole = (part * mul) >> 21
    rest = part - whole * den
    return unit * (i + whole) + ((unit * rest * mul) >> 21)


def sincos(x):
    n = jnp.floor(x * np.float32(2.0 / np.pi) + 0.5)
    r = x - n * np.float32(1.5703125)
    r = r - n * np.float32(4.837512969970703125e-4)
    r = r - n * np.float32(7.54978995489188216e-8)
    r2 = r * r
    s = r + r * r2 * (
        np.float32(-1.6666654611e-1)
        + r2 * (np.float32(8.3321608736e-3) + r2 * np.float32(-1.9515295891e-4))
    )
    c = (
        1.0
        - 0.5 * r2
        + r2 * r2 * (
            np.float32(4.166664568298827e-2)
            + r2 * (np.float32(-1.388731625493765e-3) + r2 * np.float32(2.443315711809948e-5))
        )
    )
    k = n.astype(I32)
    swap = (k & 1) == 1
    sin = jnp.where(swap, c, s)
    cos = jnp.where(swap, s, c)
    sin = jnp.where((k & 2) == 2, -sin, sin)
    cos = jnp.where(((k + 1) & 2) == 2, -cos, cos)
    return sin, cos


def dft_tables():
    turns = ((np.arange(SPOT)[:, None] - SPOT // 2) * np.arange(SUB)[None, :]) % SPOT
    angle = turns * (2.0 * np.pi / SPOT)
    c, s = np.cos(angle), -np.sin(angle)
    cols = np.concatenate([np.kron(np.eye(8), c.T), np.kron(np.eye(8), s.T)], axis=1)
    cb, sb = np.kron(np.eye(2), c), np.kron(np.eye(2), s)
    rows = np.block([[cb, -sb], [sb, cb]])
    cols_hi, cols_lo = halves(cols)
    rows_hi, rows_lo = halves(rows)
    return (
        np.concatenate([cols_hi, cols_lo, cols_hi], axis=0),
        np.concatenate([rows_hi, rows_lo, rows_hi], axis=1),
    )


def halves(a):
    a = a.astype(np.float32)
    hi = a.astype(ml_dtypes.bfloat16)
    return hi, (a - hi.astype(np.float32)).astype(ml_dtypes.bfloat16)


def split(a):
    hi = a.astype(BF16)
    return hi, (a - hi.astype(F32)).astype(BF16)


def shift_at(b, xl, k):
    px = ((b >> 4) * 2 + xl + (k & 3)) & 3
    py = ((b >> 2) + (k >> 2)) & 3
    pz = (b + (k >> 4)) & 3
    return (px >> 1) * 16 + py * 4 + pz, px & 1


def kernel(
    wind, offs, ratio, magic, screens, amp_h,
    new_out, phase, ampn,
    x, amp, send1, recv_a, recv_b, recv_c, side_s, side_r, edge_s, edge_r, y,
    relb, frac, cols, mate_a, mate_b, mate_c, rows_a, rows_b, rows_c, kidx,
    send2a, send2b, recv2a, recv2b, wbig_a, wbig_b,
    in_sem, tab_sem, s1, r1, hs, hr, ws, wr, s2, r2, osem,
):
    recv1 = (recv_a, recv_b, recv_c)
    mate, rows = (mate_a, mate_b, mate_c), (rows_a, rows_b, rows_c)
    b = lax.axis_index("layer")
    q = lax.axis_index("dir")
    xl, c = q // 2, q % 2
    chip = b * 2 + xl

    def device(pb, pxl):
        return (pb, pxl * 2 + c)

    loads = [pltpu.make_async_copy(screens.at[l], x.at[l], in_sem.at[l]) for l in range(LAYERS)]
    for load in loads:
        load.start()

    def block(db, dq):
        return ((b + db) & 31, (q + dq) & 3)

    near = [(db, dq) for db in (-1, 0, 1) for dq in (-1, 1)]
    bar = pltpu.get_barrier_semaphore()
    for n in near:
        pl.semaphore_signal(bar, inc=1, device_id=block(*n), device_id_type=MESH)

    def greet(k, _):
        pl.semaphore_signal(bar, inc=1, device_id=device(*shift_at(b, xl, 64 - k)), device_id_type=MESH)
        return 0

    lax.fori_loop(1, CHIPS, greet, 0)

    amp_load = pltpu.make_async_copy(amp_h, amp, tab_sem)
    amp_load.start()

    ro, ri = iota((BLK, BLK), 0), iota((BLK, BLK), 1)
    perm = jnp.where(ri == (ro & 7) * 64 + (ro >> 3), 1.0, 0.0).astype(BF16)

    def permute(l):
        loads[l].wait()
        ordered = jnp.dot(perm, x[l], preferred_element_type=F32)
        for t in range(4):
            send1[l, :, t] = ordered[:, t * 128:(t + 1) * 128].reshape(CHIPS, 8, 128).astype(BF16)

    def exchange(l):
        def go(k, _):
            pb, pxl = shift_at(b, xl, 64 - k)
            pltpu.make_async_remote_copy(
                src_ref=send1.at[l, pb * 2 + pxl],
                dst_ref=recv1[l].at[xl, pl.ds(b * 4, 4)],
                send_sem=s1.at[l], recv_sem=r1.at[l],
                device_id=device(pb, pxl), device_id_type=MESH,
            ).start()
            return 0

        lax.fori_loop(1, CHIPS, go, 0)
        pltpu.make_async_copy(send1.at[l, chip], recv1[l].at[xl, pl.ds(b * 4, 4)], r1.at[l]).start()

    def sent(l):
        pltpu.make_async_copy(send1.at[l, 0:63], send1.at[l, 0:63], s1.at[l]).wait()

    permute(0)
    pl.semaphore_wait(bar, 63 + len(near))
    exchange(0)
    permute(1)
    permute(2)

    lane8, row8 = iota((8, 128), 1), iota((8, 128), 0)
    first = jnp.where(lane8 == row8, 1.0, 0.0).astype(BF16)
    last = jnp.where(lane8 == row8 + 120, 1.0, 0.0).astype(BF16)
    nt = (((1,), (1,)), ((), ()))
    for l in range(LAYERS):
        side_s[0, l] = lax.dot_general(
            last, x[l, :, BLK - 128:], nt, preferred_element_type=F32).astype(BF16)
        side_s[1, l] = lax.dot_general(
            first, x[l, :, :128], nt, preferred_element_type=F32).astype(BF16)
        edge_s[0, l] = x[l, BLK - 8:]
        edge_s[1, l] = x[l, :8]

    def halo(i, src, dst, to):
        return pltpu.make_async_remote_copy(
            src_ref=src, dst_ref=dst, send_sem=hs.at[i], recv_sem=hr.at[i],
            device_id=to, device_id_type=MESH)

    halos = []
    for i, db in enumerate((1, -1)):
        dst = side_r.at[i]
        halos.append(halo(4 * i, side_s.at[i], dst.at[:, :, 128:128 + BLK], block(db, 0)))
        halos.append(halo(4 * i + 1, side_s.at[i, :, :, BLK - 128:], dst.at[:, :, :128], block(db, 1)))
        halos.append(halo(4 * i + 2, side_s.at[i, :, :, :128], dst.at[:, :, 128 + BLK:], block(db, -1)))
        halos.append(halo(4 * i + 3, edge_s.at[i], edge_r.at[i], block(0, db)))
    for h in halos:
        h.start()

    sent(0)
    exchange(1)

    def row_table(p, _):
        for l in range(LAYERS):
            for pxl in range(2):
                d = pxl * 2 + c
                num, den = ratio[l, 0, d], ratio[l, 1, d]
                r = offs[l, 0, d] - wind[0, l] + ROWS + stretch(p, NPR, num, den, magic[den])
                kidx[l, p * 2 + pxl] = ((r + ((chip - r) & 63)) & (ROWS - 1)) >> 6
        return 0

    lax.fori_loop(0, 32, row_table, 0)
    cols[...] = jnp.zeros_like(cols)

    px0 = (iota((16, 128), 0) * 128).astype(F32)
    px = px0 + iota((16, 128), 1).astype(F32)
    for d in range(DIRS):
        for l in range(LAYERS):
            num = ratio[l, 0, d].astype(F32)
            den = ratio[l, 1, d].astype(F32)
            start = (offs[l, 1, d] - wind[1, l] + COLS) & (COLS - 1)
            a = px * num
            qv = floor_div(a, den)
            tile = (start + floor_div(px0 * num, den).astype(I32)) >> 7
            relb[d * LAYERS + l] = start + qv.astype(I32) - tile * 128
            frac[d * LAYERS + l] = (a - qv * den) / den

    pupil = (b * NPR + iota((NPR, 1), 0)).astype(F32)

    def row_weights(l, mrow):
        num = ratio[l, 0, q].astype(F32)
        den = ratio[l, 1, q].astype(F32)
        start = (offs[l, 0, q] - wind[0, l] + ROWS) & (ROWS - 1)
        a = pupil * num
        qv = floor_div(a, den)
        f = (a - qv * den) / den
        base = (start + qv.astype(I32)) & 63
        high = f.astype(BF16).astype(F32)
        low = (1.0 - f).astype(BF16).astype(F32)
        return jnp.where(mrow == base, low, 0.0) + jnp.where(mrow == ((base + 1) & 63), high, 0.0)

    ca = iota((NPR, CHIPS * 24), 1)
    ma = (ca * 2731) >> 16
    ja = ca - ma * 24
    wa = jnp.where(ja < 10, row_weights(0, ma), row_weights(1, ma))
    for j in range(JT):
        wbig_a[j * NPR:(j + 1) * NPR] = jnp.where((ja == j) | (ja == j + 10), wa, 0.0).astype(BF16)
    cb = iota((NPR, CHIPS * 16), 1)
    wb = row_weights(2, cb >> 4)
    for j in range(JT):
        wbig_b[j * NPR:(j + 1) * NPR] = jnp.where((cb & 15) == j, wb, 0.0).astype(BF16)

    amp_load.wait()
    g32 = jnp.where((iota((32, 32), 0) >> 4) == (iota((32, 32), 1) >> 4), 1.0, 0.0)
    g128 = jnp.where((iota((128, 128), 0) >> 4) == (iota((128, 128), 1) >> 4), 1.0, 0.0)
    for j in range(JT):
        av = amp[:, j * 128:(j + 1) * 128]
        energy = jnp.dot(g32, av * av, precision=HIGHEST, preferred_element_type=F32)
        energy = jnp.dot(energy, g128, precision=HIGHEST, preferred_element_type=F32)
        ampn[j] = av / jnp.sqrt(energy)

    sent(1)
    exchange(2)
    for h in halos:
        h.wait()
    tn = (((0,), (0,)), ((), ()))
    for l in range(LAYERS):
        w0, w1 = wind[0, l], wind[1, l]
        left = lax.dot_general(side_r[0, l], last, tn, preferred_element_type=F32)
        right = lax.dot_general(side_r[1, l], first, tn, preferred_element_type=F32)
        for r0, n, src in ((0, 8, edge_r.at[0, l]), (8, BLK, x.at[l]), (BLK + 8, 8, edge_r.at[1, l])):
            at = r0 + 120
            lanes = [left[at:at + n]]
            lanes += [src[:, t * 128:(t + 1) * 128].astype(F32) for t in range(4)]
            lanes += [right[at:at + n]]
            turned = [pltpu.roll(v, (w1 + 128) & 127, 1) for v in lanes]
            lane = iota((n, 128), 1)
            before, after = lane < w1, lane >= 128 + w1
            for t in range(4):
                y[r0:r0 + n, t * 128:(t + 1) * 128] = jnp.where(
                    before, turned[t], jnp.where(after, turned[t + 2], turned[t + 1]))
        turn, whole = w0 & 7, w0 >> 3
        keep = iota((BLK // 8 + 1, 8, 128), 1) >= turn
        for t in range(4):
            part = y[:, t * 128:(t + 1) * 128].reshape(BLK // 8 + 2, 8, 128)
            part = pltpu.roll(part, turn, 1)
            part = jnp.concatenate([part[:1], jnp.where(keep, part[1:], part[:-1])], axis=0)
            val = jnp.where(whole > 0, part[:-2], jnp.where(whole == 0, part[1:-1], part[2:]))
            x[l, :, t * 128:(t + 1) * 128] = val.reshape(BLK, 128).astype(BF16)
        pltpu.make_async_copy(x.at[l], new_out.at[l], osem.at[l]).start()

    def columns(l):
        def one(d, j):
            num, den = ratio[l, 0, d], ratio[l, 1, d]
            start = (offs[l, 1, d] - wind[1, l] + COLS) & (COLS - 1)
            tile = (start + stretch(j, 128, num, den, magic[den])) >> 7
            rel = relb[d * LAYERS + l, pl.ds(j, 1), :]
            f = frac[d * LAYERS + l, pl.ds(j, 1), :]
            high = f.astype(BF16).astype(F32)
            low = (1.0 - f).astype(BF16).astype(F32)
            rel = jnp.broadcast_to(rel, (8, 128))
            rel_u = rel + 1
            idx, idx_u = rel & 127, rel_u & 127
            sel, sel_u = rel >> 7, rel_u >> 7
            for h in range(2):
                t = [recv1[l][h, (tile + s) & 127].astype(F32) for s in range(3)]
                g = [jnp.take_along_axis(v, idx, axis=1) for v in t]
                u = [jnp.take_along_axis(v, idx_u, axis=1) for v in t]
                vb = jnp.where(sel == 0, g[0], jnp.where(sel == 1, g[1], g[2]))
                vu = jnp.where(sel_u == 0, u[0], jnp.where(sel_u == 1, u[1], u[2]))
                out = low * vb + high * vu
                cols.at[d % 2, d // 2, h].reshape(128, 128)[pl.ds(j, 8, stride=16), :] = out

        def direction(d, _):
            for j in range(JT):
                one(d, j)
            return 0

        lax.fori_loop(0, DIRS, direction, 0)
        mate[l][...] = cols[1 - c].astype(BF16)
        rows[l][c] = cols[c].astype(BF16)

    def swap(l):
        return pltpu.make_async_remote_copy(
            src_ref=mate[l], dst_ref=rows[l].at[c],
            send_sem=ws.at[l], recv_sem=wr.at[l],
            device_id=(b, xl * 2 + 1 - c), device_id_type=MESH)

    def arrive(l):
        pltpu.make_async_copy(recv1[l], recv1[l], r1.at[l]).wait()
        columns(l)
        swap(l).start()

    def row_of(l, dest):
        k = kidx[l, dest]
        return rows[l][(k >> 3) & 1, dest & 1, k >> 4, k & 7]

    sub = iota((8, 128), 0)

    def pack_a(dest):
        val_a, val_b = row_of(0, dest).astype(F32), row_of(1, dest).astype(F32)
        b0, b1 = pltpu.roll(val_b[:8], 2, 0), pltpu.roll(val_b[8:], 2, 0)
        send2a[dest, 0] = val_a[:8].astype(BF16)
        send2a[dest, 1] = jnp.where(sub < 2, val_a[8:], b0).astype(BF16)
        send2a[dest, 2] = jnp.where(sub < 2, b0, b1).astype(BF16)

    def pack_b(dest):
        send2b[dest] = row_of(2, dest)

    def deliver(i, src, dst, pack):
        def some(n, _):
            for u in range(7):
                pb, pxl = shift_at(b, xl, 63 - n * 7 - u)
                pack(pb * 2 + pxl)
            for u in range(7):
                pb, pxl = shift_at(b, xl, 63 - n * 7 - u)
                pltpu.make_async_remote_copy(
                    src_ref=src.at[pb * 2 + pxl], dst_ref=dst.at[chip],
                    send_sem=s2.at[i], recv_sem=r2.at[i],
                    device_id=device(pb, pxl), device_id_type=MESH,
                ).start()
            return 0

        lax.fori_loop(0, 9, some, 0)
        pack(chip)
        pltpu.make_async_copy(src.at[chip], dst.at[chip], r2.at[i]).start()

    arrive(0)
    arrive(1)
    swap(0).wait()
    swap(1).wait()
    deliver(0, send2a, recv2a, pack_a)
    arrive(2)
    swap(2).wait()
    deliver(1, send2b, recv2b, pack_b)

    pltpu.make_async_copy(recv2a, recv2a, r2.at[0]).wait()
    phase[...] = jnp.dot(
        wbig_a[...], recv2a[...].reshape(CHIPS * 24, 128), preferred_element_type=F32)
    pltpu.make_async_copy(recv2b, recv2b, r2.at[1]).wait()
    phase[...] += jnp.dot(
        wbig_b[...], recv2b[...].reshape(CHIPS * 16, 128), preferred_element_type=F32)

    for l in range(LAYERS):
        pltpu.make_async_copy(x.at[l], new_out.at[l], osem.at[l]).wait()
    sent(2)
    pltpu.make_async_copy(send2a.at[0:63], send2a.at[0:63], s2.at[0]).wait()
    pltpu.make_async_copy(send2b.at[0:63], send2b.at[0:63], s2.at[1]).wait()


def image(phase, ampn, dcol, drow, new_in, new_out, spots, field, half, out, nsem, osem):
    copy = pltpu.make_async_copy(new_in, new_out, nsem)
    copy.start()
    for j in range(JT):
        sin, cos = sincos(phase[j * NPR:(j + 1) * NPR])
        for i, v in enumerate((ampn[j] * cos, ampn[j] * sin)):
            hi, lo = split(v)
            at = j * 64 + i * 32
            field[at:at + 32, :128] = hi
            field[at:at + 32, 128:256] = hi
            field[at:at + 32, 256:] = lo
    half[...] = jnp.dot(field[...], dcol[...], preferred_element_type=F32)
    stores = []
    for j in range(JT):
        g = half[j * 64:(j + 1) * 64]
        re = split(g[:32, :256] - g[32:, 256:])
        im = split(g[:32, 256:] + g[32:, :256])
        data = jnp.concatenate([re[0], im[0], re[0], im[0], re[1], im[1]], axis=0)
        full = jnp.dot(drow[...], data, preferred_element_type=F32)
        out[:, j * 256:(j + 1) * 256] = full[:64] * full[:64] + full[64:] * full[64:]
        store = pltpu.make_async_copy(
            out.at[:, j * 256:(j + 1) * 256], spots.at[:, j * 256:(j + 1) * 256], osem.at[j])
        store.start()
        stores.append(store)
    for store in stores:
        store.wait()
    copy.wait()


def per_device(screens, amplitude, wind, offsets, ratio):
    dcol, drow = dft_tables()
    vmem = pl.BlockSpec(memory_space=pltpu.VMEM)
    smem = pl.BlockSpec(memory_space=pltpu.SMEM)
    hbm = pl.BlockSpec(memory_space=pltpu.HBM)
    anywhere = pl.BlockSpec(memory_space=pl.ANY)
    dma = pltpu.SemaphoreType.DMA
    new, phase, ampn = pl.pallas_call(
        kernel,
        out_shape=(
            jax.ShapeDtypeStruct((LAYERS, BLK, BLK), BF16),
            jax.ShapeDtypeStruct((JT * NPR, 128), F32),
            jax.ShapeDtypeStruct((JT, NPR, 128), F32),
        ),
        in_specs=[smem, smem, smem, smem, hbm, hbm],
        out_specs=(anywhere, vmem, vmem),
        scratch_shapes=[
            pltpu.VMEM((LAYERS, BLK, BLK), BF16),
            pltpu.VMEM((NPR, PC), F32),
            pltpu.VMEM((LAYERS, CHIPS, 4, 8, 128), BF16),
            pltpu.VMEM((2, 128, 8, 128), BF16),
            pltpu.VMEM((2, 128, 8, 128), BF16),
            pltpu.VMEM((2, 128, 8, 128), BF16),
            pltpu.VMEM((2, LAYERS, 8, BLK), BF16),
            pltpu.VMEM((2, LAYERS, 8, BLK + 256), BF16),
            pltpu.VMEM((2, LAYERS, 8, BLK), BF16),
            pltpu.VMEM((2, LAYERS, 8, BLK), BF16),
            pltpu.VMEM((BLK + 16, BLK), F32),
            pltpu.VMEM((DIRS * LAYERS, 16, 128), I32),
            pltpu.VMEM((DIRS * LAYERS, 16, 128), F32),
            pltpu.VMEM((2, 2, 2, 8, 16, 128), F32),
            *[pltpu.VMEM((2, 2, 8, 16, 128), BF16)] * 3,
            *[pltpu.VMEM((2, 2, 2, 8, 16, 128), BF16)] * 3,
            pltpu.SMEM((LAYERS, CHIPS), I32),
            pltpu.VMEM((CHIPS, 3, 8, 128), BF16),
            pltpu.VMEM((CHIPS, 16, 128), BF16),
            pltpu.VMEM((CHIPS, 3, 8, 128), BF16),
            pltpu.VMEM((CHIPS, 16, 128), BF16),
            pltpu.VMEM((JT * NPR, CHIPS * 24), BF16),
            pltpu.VMEM((JT * NPR, CHIPS * 16), BF16),
            dma((3,)), dma, dma((3,)), dma((3,)), dma((8,)), dma((8,)),
            dma((3,)), dma((3,)), dma((2,)), dma((2,)), dma((3,)),
        ],
        compiler_params=pltpu.CompilerParams(
            collective_id=0, has_side_effects=True, vmem_limit_bytes=32 << 20),
        name="screens_to_phase",
    )(
        *[
            pltpu.with_memory_space_constraint(v, pltpu.HBM)
            for v in (
                wind.T, offsets.transpose(1, 2, 0), ratio.transpose(1, 2, 0),
                jnp.asarray(reciprocals()), screens, amplitude,
            )
        ]
    )
    new, spots = pl.pallas_call(
        image,
        out_shape=(
            jax.ShapeDtypeStruct((LAYERS, BLK, BLK), BF16),
            jax.ShapeDtypeStruct((64, 2560), F32),
        ),
        in_specs=[vmem, vmem, vmem, vmem, anywhere],
        out_specs=(hbm, hbm),
        scratch_shapes=[
            pltpu.VMEM((JT * 64, 384), BF16),
            pltpu.VMEM((JT * 64, 512), F32),
            pltpu.VMEM((64, 2560), F32),
            dma, dma((JT,)),
        ],
        compiler_params=pltpu.CompilerParams(vmem_limit_bytes=32 << 20),
        name="phase_to_spots",
    )(phase, ampn, jnp.asarray(dcol), jnp.asarray(drow), new)
    return new, spots[None]


def solution(mesh):
    return jax.shard_map(
        per_device,
        mesh=mesh,
        in_specs=(P(None, "dir", "layer"), P("layer", None), P(), P(), P()),
        out_specs=(P(None, "dir", "layer"), P("dir", "layer", None)),
        check_vma=False,
    )
```

```python
import jax
import jax.numpy as jnp
import ml_dtypes
import numpy as np
from jax import lax
from jax.experimental import pallas as pl
from jax.experimental.pallas import tpu as pltpu
from jax.sharding import PartitionSpec as P

MESH = pl.DeviceIdType.MESH
SUB = 16
SPOT = 32
HALO = 8
LAYERS = 3
DIRS = 4
ROWS, COLS = 2048, 16384
PR, PC = 1024, 1280
BLK = 512
CHIPS = 64
JT = PC // 128
NPR = 32
F32, BF16, I32 = jnp.float32, jnp.bfloat16, jnp.int32
HIGHEST = lax.Precision.HIGHEST


def iota(shape, dim):
    return lax.broadcasted_iota(I32, shape, dim)


def floor_div(a, den):
    q = jnp.floor(a / den)
    r = a - q * den
    q = q + jnp.where(r >= den, 1.0, 0.0) - jnp.where(r < 0.0, 1.0, 0.0)
    return q


def reciprocals():
    den = np.maximum(np.arange(129), 1)
    return (2 ** 21 // den + 1).astype(np.int32)


def stretch(i, unit, num, den, mul):
    part = i * (num - den)
    whole = (part * mul) >> 21
    rest = part - whole * den
    return unit * (i + whole) + ((unit * rest * mul) >> 21)


def sincos(x):
    n = jnp.floor(x * np.float32(2.0 / np.pi) + 0.5)
    r = x - n * np.float32(1.5703125)
    r = r - n * np.float32(4.837512969970703125e-4)
    r = r - n * np.float32(7.54978995489188216e-8)
    r2 = r * r
    s = r + r * r2 * (
        np.float32(-1.6666654611e-1)
        + r2 * (np.float32(8.3321608736e-3) + r2 * np.float32(-1.9515295891e-4))
    )
    c = (
        1.0
        - 0.5 * r2
        + r2 * r2 * (
            np.float32(4.166664568298827e-2)
            + r2 * (np.float32(-1.388731625493765e-3) + r2 * np.float32(2.443315711809948e-5))
        )
    )
    k = n.astype(I32)
    swap = (k & 1) == 1
    sin = jnp.where(swap, c, s)
    cos = jnp.where(swap, s, c)
    sin = jnp.where((k & 2) == 2, -sin, sin)
    cos = jnp.where(((k + 1) & 2) == 2, -cos, cos)
    return sin, cos


def dft_tables():
    turns = ((np.arange(SPOT)[:, None] - SPOT // 2) * np.arange(SUB)[None, :]) % SPOT
    angle = turns * (2.0 * np.pi / SPOT)
    c, s = np.cos(angle), -np.sin(angle)
    cols = np.concatenate([np.kron(np.eye(8), c.T), np.kron(np.eye(8), s.T)], axis=1)
    cb, sb = np.kron(np.eye(2), c), np.kron(np.eye(2), s)
    rows = np.block([[cb, -sb], [sb, cb]])
    cols_hi, cols_lo = halves(cols)
    rows_hi, rows_lo = halves(rows)
    return (
        np.concatenate([cols_hi, cols_lo, cols_hi], axis=0),
        np.concatenate([rows_hi, rows_lo, rows_hi], axis=1),
    )


def halves(a):
    a = a.astype(np.float32)
    hi = a.astype(ml_dtypes.bfloat16)
    return hi, (a - hi.astype(np.float32)).astype(ml_dtypes.bfloat16)


def split(a):
    hi = a.astype(BF16)
    return hi, (a - hi.astype(F32)).astype(BF16)


def shift_at(b, xl, k):
    px = ((b >> 4) * 2 + xl + (k & 3)) & 3
    py = ((b >> 2) + (k >> 2)) & 3
    pz = (b + (k >> 4)) & 3
    return (px >> 1) * 16 + py * 4 + pz, px & 1


def kernel(
    wind, offs, ratio, magic, screens, amp_h,
    new_out, phase, ampn,
    x, amp, send1, recv_a, recv_b, recv_c, side_s, side_r, edge_s, edge_r, y,
    relb, frac, cols, mate_a, mate_b, mate_c, rows_a, rows_b, rows_c, kidx,
    send2a, send2b, recv2a, recv2b, wbig_a, wbig_b,
    in_sem, tab_sem, s1, r1, hs, hr, ws, wr, s2, r2, osem,
):
    recv1 = (recv_a, recv_b, recv_c)
    mate, rows = (mate_a, mate_b, mate_c), (rows_a, rows_b, rows_c)
    b = lax.axis_index("layer")
    q = lax.axis_index("dir")
    xl, c = q // 2, q % 2
    chip = b * 2 + xl

    def device(pb, pxl):
        return (pb, pxl * 2 + c)

    loads = [pltpu.make_async_copy(screens.at[l], x.at[l], in_sem.at[l]) for l in range(LAYERS)]
    for load in loads:
        load.start()

    def block(db, dq):
        return ((b + db) & 31, (q + dq) & 3)

    near = [(db, dq) for db in (-1, 0, 1) for dq in (-1, 1)]
    bar = pltpu.get_barrier_semaphore()
    for n in near:
        pl.semaphore_signal(bar, inc=1, device_id=block(*n), device_id_type=MESH)

    def greet(k, _):
        pl.semaphore_signal(bar, inc=1, device_id=device(*shift_at(b, xl, 64 - k)), device_id_type=MESH)
        return 0

    lax.fori_loop(1, CHIPS, greet, 0)

    amp_load = pltpu.make_async_copy(amp_h, amp, tab_sem)
    amp_load.start()

    ro, ri = iota((BLK, BLK), 0), iota((BLK, BLK), 1)
    perm = jnp.where(ri == (ro & 7) * 64 + (ro >> 3), 1.0, 0.0).astype(BF16)

    def permute(l):
        loads[l].wait()
        ordered = jnp.dot(perm, x[l], preferred_element_type=F32)
        for t in range(4):
            send1[l, :, t] = ordered[:, t * 128:(t + 1) * 128].reshape(CHIPS, 8, 128).astype(BF16)

    def exchange(l):
        def go(k, _):
            pb, pxl = shift_at(b, xl, 64 - k)
            pltpu.make_async_remote_copy(
                src_ref=send1.at[l, pb * 2 + pxl],
                dst_ref=recv1[l].at[xl, pl.ds(b * 4, 4)],
                send_sem=s1.at[l], recv_sem=r1.at[l],
                device_id=device(pb, pxl), device_id_type=MESH,
            ).start()
            return 0

        lax.fori_loop(1, CHIPS, go, 0)
        pltpu.make_async_copy(send1.at[l, chip], recv1[l].at[xl, pl.ds(b * 4, 4)], r1.at[l]).start()

    def sent(l):
        pltpu.make_async_copy(send1.at[l, 0:63], send1.at[l, 0:63], s1.at[l]).wait()

    permute(0)
    pl.semaphore_wait(bar, 63 + len(near))
    exchange(0)
    permute(1)
    permute(2)

    lane8, row8 = iota((8, 128), 1), iota((8, 128), 0)
    first = jnp.where(lane8 == row8, 1.0, 0.0).astype(BF16)
    last = jnp.where(lane8 == row8 + 120, 1.0, 0.0).astype(BF16)
    nt = (((1,), (1,)), ((), ()))
    for l in range(LAYERS):
        side_s[0, l] = lax.dot_general(
            last, x[l, :, BLK - 128:], nt, preferred_element_type=F32).astype(BF16)
        side_s[1, l] = lax.dot_general(
            first, x[l, :, :128], nt, preferred_element_type=F32).astype(BF16)
        edge_s[0, l] = x[l, BLK - 8:]
        edge_s[1, l] = x[l, :8]

    def halo(i, src, dst, to):
        return pltpu.make_async_remote_copy(
            src_ref=src, dst_ref=dst, send_sem=hs.at[i], recv_sem=hr.at[i],
            device_id=to, device_id_type=MESH)

    halos = []
    for i, db in enumerate((1, -1)):
        dst = side_r.at[i]
        halos.append(halo(4 * i, side_s.at[i], dst.at[:, :, 128:128 + BLK], block(db, 0)))
        halos.append(halo(4 * i + 1, side_s.at[i, :, :, BLK - 128:], dst.at[:, :, :128], block(db, 1)))
        halos.append(halo(4 * i + 2, side_s.at[i, :, :, :128], dst.at[:, :, 128 + BLK:], block(db, -1)))
        halos.append(halo(4 * i + 3, edge_s.at[i], edge_r.at[i], block(0, db)))
    for h in halos:
        h.start()

    sent(0)
    exchange(1)

    def row_table(p, _):
        for l in range(LAYERS):
            for pxl in range(2):
                d = pxl * 2 + c
                num, den = ratio[l, 0, d], ratio[l, 1, d]
                r = offs[l, 0, d] - wind[0, l] + ROWS + stretch(p, NPR, num, den, magic[den])
                kidx[l, p * 2 + pxl] = ((r + ((chip - r) & 63)) & (ROWS - 1)) >> 6
        return 0

    lax.fori_loop(0, 32, row_table, 0)
    cols[...] = jnp.zeros_like(cols)

    px0 = (iota((16, 128), 0) * 128).astype(F32)
    px = px0 + iota((16, 128), 1).astype(F32)
    for d in range(DIRS):
        for l in range(LAYERS):
            num = ratio[l, 0, d].astype(F32)
            den = ratio[l, 1, d].astype(F32)
            start = (offs[l, 1, d] - wind[1, l] + COLS) & (COLS - 1)
            a = px * num
            qv = floor_div(a, den)
            tile = (start + floor_div(px0 * num, den).astype(I32)) >> 7
            relb[d * LAYERS + l] = start + qv.astype(I32) - tile * 128
            frac[d * LAYERS + l] = (a - qv * den) / den

    pupil = (b * NPR + iota((NPR, 1), 0)).astype(F32)

    def row_weights(l, mrow):
        num = ratio[l, 0, q].astype(F32)
        den = ratio[l, 1, q].astype(F32)
        start = (offs[l, 0, q] - wind[0, l] + ROWS) & (ROWS - 1)
        a = pupil * num
        qv = floor_div(a, den)
        f = (a - qv * den) / den
        base = (start + qv.astype(I32)) & 63
        high = f.astype(BF16).astype(F32)
        low = (1.0 - f).astype(BF16).astype(F32)
        return jnp.where(mrow == base, low, 0.0) + jnp.where(mrow == ((base + 1) & 63), high, 0.0)

    cc = iota((NPR, CHIPS * 16), 1)
    m, r = cc >> 4, cc & 15
    w0, w1, w2 = [row_weights(l, m) for l in range(LAYERS)]
    wa, wb = jnp.where(r < 10, w0, w1), jnp.where(r < 4, w1, w2)
    for j in range(JT):
        in_a, in_b = r == j, (r == j + 4) & (r >= 4)
        if j < 6:
            in_a = in_a | (r == j + 10)
        else:
            in_b = in_b | (r == j - 6)
        wbig_a[j * NPR:(j + 1) * NPR] = jnp.where(in_a, wa, 0.0).astype(BF16)
        wbig_b[j * NPR:(j + 1) * NPR] = jnp.where(in_b, wb, 0.0).astype(BF16)

    amp_load.wait()
    g32 = jnp.where((iota((32, 32), 0) >> 4) == (iota((32, 32), 1) >> 4), 1.0, 0.0)
    g128 = jnp.where((iota((128, 128), 0) >> 4) == (iota((128, 128), 1) >> 4), 1.0, 0.0)
    for j in range(JT):
        av = amp[:, j * 128:(j + 1) * 128]
        energy = jnp.dot(g32, av * av, precision=HIGHEST, preferred_element_type=F32)
        energy = jnp.dot(energy, g128, precision=HIGHEST, preferred_element_type=F32)
        ampn[j] = av / jnp.sqrt(energy)

    sent(1)
    exchange(2)
    for h in halos:
        h.wait()
    tn = (((0,), (0,)), ((), ()))
    for l in range(LAYERS):
        w0, w1 = wind[0, l], wind[1, l]
        left = lax.dot_general(side_r[0, l], last, tn, preferred_element_type=F32)
        right = lax.dot_general(side_r[1, l], first, tn, preferred_element_type=F32)
        for r0, n, src in ((0, 8, edge_r.at[0, l]), (8, BLK, x.at[l]), (BLK + 8, 8, edge_r.at[1, l])):
            at = r0 + 120
            lanes = [left[at:at + n]]
            lanes += [src[:, t * 128:(t + 1) * 128].astype(F32) for t in range(4)]
            lanes += [right[at:at + n]]
            turned = [pltpu.roll(v, (w1 + 128) & 127, 1) for v in lanes]
            lane = iota((n, 128), 1)
            before, after = lane < w1, lane >= 128 + w1
            for t in range(4):
                y[r0:r0 + n, t * 128:(t + 1) * 128] = jnp.where(
                    before, turned[t], jnp.where(after, turned[t + 2], turned[t + 1]))
        turn, whole = w0 & 7, w0 >> 3
        keep = iota((BLK // 8 + 1, 8, 128), 1) >= turn
        for t in range(4):
            part = y[:, t * 128:(t + 1) * 128].reshape(BLK // 8 + 2, 8, 128)
            part = pltpu.roll(part, turn, 1)
            part = jnp.concatenate([part[:1], jnp.where(keep, part[1:], part[:-1])], axis=0)
            val = jnp.where(whole > 0, part[:-2], jnp.where(whole == 0, part[1:-1], part[2:]))
            x[l, :, t * 128:(t + 1) * 128] = val.reshape(BLK, 128).astype(BF16)
        pltpu.make_async_copy(x.at[l], new_out.at[l], osem.at[l]).start()

    def columns(l):
        def one(d, j):
            num, den = ratio[l, 0, d], ratio[l, 1, d]
            start = (offs[l, 1, d] - wind[1, l] + COLS) & (COLS - 1)
            tile = (start + stretch(j, 128, num, den, magic[den])) >> 7
            rel = relb[d * LAYERS + l, pl.ds(j, 1), :]
            f = frac[d * LAYERS + l, pl.ds(j, 1), :]
            high = f.astype(BF16).astype(F32)
            low = (1.0 - f).astype(BF16).astype(F32)
            rel = jnp.broadcast_to(rel, (8, 128))
            rel_u = rel + 1
            idx, idx_u = rel & 127, rel_u & 127
            sel, sel_u = rel >> 7, rel_u >> 7
            for h in range(2):
                t = [recv1[l][h, (tile + s) & 127].astype(F32) for s in range(3)]
                g = [jnp.take_along_axis(v, idx, axis=1) for v in t]
                u = [jnp.take_along_axis(v, idx_u, axis=1) for v in t]
                vb = jnp.where(sel == 0, g[0], jnp.where(sel == 1, g[1], g[2]))
                vu = jnp.where(sel_u == 0, u[0], jnp.where(sel_u == 1, u[1], u[2]))
                out = low * vb + high * vu
                cols.at[d % 2, d // 2, h].reshape(128, 128)[pl.ds(j, 8, stride=16), :] = out

        def direction(d, _):
            for j in range(JT):
                one(d, j)
            return 0

        lax.fori_loop(0, DIRS, direction, 0)
        mate[l][...] = cols[1 - c].astype(BF16)
        rows[l][c] = cols[c].astype(BF16)

    def swap(l):
        return pltpu.make_async_remote_copy(
            src_ref=mate[l], dst_ref=rows[l].at[c],
            send_sem=ws.at[l], recv_sem=wr.at[l],
            device_id=(b, xl * 2 + 1 - c), device_id_type=MESH)

    def arrive(l):
        pltpu.make_async_copy(recv1[l], recv1[l], r1.at[l]).wait()
        columns(l)
        swap(l).start()

    def row_of(l, dest):
        k = kidx[l, dest]
        return rows[l][(k >> 3) & 1, dest & 1, k >> 4, k & 7]

    sub = iota((8, 128), 0)

    def turn_rows(v, n):
        return pltpu.roll(v[:8], n, 0), pltpu.roll(v[8:], n, 0)

    def pack_a(dest):
        a, b0 = row_of(0, dest).astype(F32), row_of(1, dest).astype(F32)
        t0, _ = turn_rows(b0, 2)
        send2a[dest] = jnp.concatenate([a[:8], jnp.where(sub < 2, a[8:], t0)], axis=0).astype(BF16)

    def pack_b(dest):
        t0, t1 = turn_rows(row_of(1, dest).astype(F32), 2)
        u0, u1 = turn_rows(row_of(2, dest).astype(F32), 4)
        top = jnp.where(sub < 2, t0, jnp.where(sub < 4, t1, u0))
        send2b[dest] = jnp.concatenate([top, jnp.where(sub < 4, u0, u1)], axis=0).astype(BF16)

    def deliver(i, src, dst, pack):
        def some(n, _):
            for u in range(7):
                pb, pxl = shift_at(b, xl, 63 - n * 7 - u)
                pack(pb * 2 + pxl)
            for u in range(7):
                pb, pxl = shift_at(b, xl, 63 - n * 7 - u)
                pltpu.make_async_remote_copy(
                    src_ref=src.at[pb * 2 + pxl], dst_ref=dst.at[chip],
                    send_sem=s2.at[i], recv_sem=r2.at[i],
                    device_id=device(pb, pxl), device_id_type=MESH,
                ).start()
            return 0

        lax.fori_loop(0, 9, some, 0)
        pack(chip)
        pltpu.make_async_copy(src.at[chip], dst.at[chip], r2.at[i]).start()

    arrive(0)
    arrive(1)
    swap(0).wait()
    swap(1).wait()
    deliver(0, send2a, recv2a, pack_a)
    arrive(2)
    swap(2).wait()
    deliver(1, send2b, recv2b, pack_b)

    pltpu.make_async_copy(recv2a, recv2a, r2.at[0]).wait()
    phase[...] = jnp.dot(
        wbig_a[...], recv2a[...].reshape(CHIPS * 16, 128), preferred_element_type=F32)
    pltpu.make_async_copy(recv2b, recv2b, r2.at[1]).wait()
    phase[...] += jnp.dot(
        wbig_b[...], recv2b[...].reshape(CHIPS * 16, 128), preferred_element_type=F32)

    for l in range(LAYERS):
        pltpu.make_async_copy(x.at[l], new_out.at[l], osem.at[l]).wait()
    sent(2)
    pltpu.make_async_copy(send2a.at[0:63], send2a.at[0:63], s2.at[0]).wait()
    pltpu.make_async_copy(send2b.at[0:63], send2b.at[0:63], s2.at[1]).wait()


def image(phase, ampn, dcol, drow, new_in, new_out, spots, field, half, out, nsem, osem):
    copy = pltpu.make_async_copy(new_in, new_out, nsem)
    copy.start()
    for j in range(JT):
        sin, cos = sincos(phase[j * NPR:(j + 1) * NPR])
        for i, v in enumerate((ampn[j] * cos, ampn[j] * sin)):
            hi, lo = split(v)
            at = j * 64 + i * 32
            field[at:at + 32, :128] = hi
            field[at:at + 32, 128:256] = hi
            field[at:at + 32, 256:] = lo
    half[...] = jnp.dot(field[...], dcol[...], preferred_element_type=F32)
    stores = []
    for j in range(JT):
        g = half[j * 64:(j + 1) * 64]
        re = split(g[:32, :256] - g[32:, 256:])
        im = split(g[:32, 256:] + g[32:, :256])
        data = jnp.concatenate([re[0], im[0], re[0], im[0], re[1], im[1]], axis=0)
        full = jnp.dot(drow[...], data, preferred_element_type=F32)
        out[:, j * 256:(j + 1) * 256] = full[:64] * full[:64] + full[64:] * full[64:]
        store = pltpu.make_async_copy(
            out.at[:, j * 256:(j + 1) * 256], spots.at[:, j * 256:(j + 1) * 256], osem.at[j])
        store.start()
        stores.append(store)
    for store in stores:
        store.wait()
    copy.wait()


def per_device(screens, amplitude, wind, offsets, ratio):
    dcol, drow = dft_tables()
    vmem = pl.BlockSpec(memory_space=pltpu.VMEM)
    smem = pl.BlockSpec(memory_space=pltpu.SMEM)
    hbm = pl.BlockSpec(memory_space=pltpu.HBM)
    anywhere = pl.BlockSpec(memory_space=pl.ANY)
    dma = pltpu.SemaphoreType.DMA
    new, phase, ampn = pl.pallas_call(
        kernel,
        out_shape=(
            jax.ShapeDtypeStruct((LAYERS, BLK, BLK), BF16),
            jax.ShapeDtypeStruct((JT * NPR, 128), F32),
            jax.ShapeDtypeStruct((JT, NPR, 128), F32),
        ),
        in_specs=[smem, smem, smem, smem, hbm, hbm],
        out_specs=(anywhere, vmem, vmem),
        scratch_shapes=[
            pltpu.VMEM((LAYERS, BLK, BLK), BF16),
            pltpu.VMEM((NPR, PC), F32),
            pltpu.VMEM((LAYERS, CHIPS, 4, 8, 128), BF16),
            pltpu.VMEM((2, 128, 8, 128), BF16),
            pltpu.VMEM((2, 128, 8, 128), BF16),
            pltpu.VMEM((2, 128, 8, 128), BF16),
            pltpu.VMEM((2, LAYERS, 8, BLK), BF16),
            pltpu.VMEM((2, LAYERS, 8, BLK + 256), BF16),
            pltpu.VMEM((2, LAYERS, 8, BLK), BF16),
            pltpu.VMEM((2, LAYERS, 8, BLK), BF16),
            pltpu.VMEM((BLK + 16, BLK), F32),
            pltpu.VMEM((DIRS * LAYERS, 16, 128), I32),
            pltpu.VMEM((DIRS * LAYERS, 16, 128), F32),
            pltpu.VMEM((2, 2, 2, 8, 16, 128), F32),
            *[pltpu.VMEM((2, 2, 8, 16, 128), BF16)] * 3,
            *[pltpu.VMEM((2, 2, 2, 8, 16, 128), BF16)] * 3,
            pltpu.SMEM((LAYERS, CHIPS), I32),
            pltpu.VMEM((CHIPS, 16, 128), BF16),
            pltpu.VMEM((CHIPS, 16, 128), BF16),
            pltpu.VMEM((CHIPS, 16, 128), BF16),
            pltpu.VMEM((CHIPS, 16, 128), BF16),
            pltpu.VMEM((JT * NPR, CHIPS * 16), BF16),
            pltpu.VMEM((JT * NPR, CHIPS * 16), BF16),
            dma((3,)), dma, dma((3,)), dma((3,)), dma((8,)), dma((8,)),
            dma((3,)), dma((3,)), dma((2,)), dma((2,)), dma((3,)),
        ],
        compiler_params=pltpu.CompilerParams(
            collective_id=0, has_side_effects=True, vmem_limit_bytes=32 << 20),
        name="screens_to_phase",
    )(
        *[
            pltpu.with_memory_space_constraint(v, pltpu.HBM)
            for v in (
                wind.T, offsets.transpose(1, 2, 0), ratio.transpose(1, 2, 0),
                jnp.asarray(reciprocals()), screens, amplitude,
            )
        ]
    )
    new, spots = pl.pallas_call(
        image,
        out_shape=(
            jax.ShapeDtypeStruct((LAYERS, BLK, BLK), BF16),
            jax.ShapeDtypeStruct((64, 2560), F32),
        ),
        in_specs=[vmem, vmem, vmem, vmem, anywhere],
        out_specs=(hbm, hbm),
        scratch_shapes=[
            pltpu.VMEM((JT * 64, 384), BF16),
            pltpu.VMEM((JT * 64, 512), F32),
            pltpu.VMEM((64, 2560), F32),
            dma, dma((JT,)),
        ],
        compiler_params=pltpu.CompilerParams(vmem_limit_bytes=32 << 20),
        name="phase_to_spots",
    )(phase, ampn, jnp.asarray(dcol), jnp.asarray(drow), new)
    return new, spots[None]


def solution(mesh):
    return jax.shard_map(
        per_device,
        mesh=mesh,
        in_specs=(P(None, "dir", "layer"), P("layer", None), P(), P(), P()),
        out_specs=(P(None, "dir", "layer"), P("dir", "layer", None)),
        check_vma=False,
    )
```

```python
import jax
import jax.numpy as jnp
import ml_dtypes
import numpy as np
from jax import lax
from jax.experimental import pallas as pl
from jax.experimental.pallas import tpu as pltpu
from jax.sharding import PartitionSpec as P

MESH = pl.DeviceIdType.MESH
SUB = 16
SPOT = 32
HALO = 8
LAYERS = 3
DIRS = 4
ROWS, COLS = 2048, 16384
PR, PC = 1024, 1280
BLK = 512
CHIPS = 64
JT = PC // 128
NPR = 32
F32, BF16, I32 = jnp.float32, jnp.bfloat16, jnp.int32
HIGHEST = lax.Precision.HIGHEST


def iota(shape, dim):
    return lax.broadcasted_iota(I32, shape, dim)


def floor_div(a, den):
    q = jnp.floor(a / den)
    r = a - q * den
    q = q + jnp.where(r >= den, 1.0, 0.0) - jnp.where(r < 0.0, 1.0, 0.0)
    return q


def reciprocals():
    den = np.maximum(np.arange(129), 1)
    return (2 ** 21 // den + 1).astype(np.int32)


def stretch(i, unit, num, den, mul):
    part = i * (num - den)
    whole = (part * mul) >> 21
    rest = part - whole * den
    return unit * (i + whole) + ((unit * rest * mul) >> 21)


def sincos(x):
    n = jnp.floor(x * np.float32(2.0 / np.pi) + 0.5)
    r = x - n * np.float32(1.5703125)
    r = r - n * np.float32(4.837512969970703125e-4)
    r = r - n * np.float32(7.54978995489188216e-8)
    r2 = r * r
    s = r + r * r2 * (
        np.float32(-1.6666654611e-1)
        + r2 * (np.float32(8.3321608736e-3) + r2 * np.float32(-1.9515295891e-4))
    )
    c = (
        1.0
        - 0.5 * r2
        + r2 * r2 * (
            np.float32(4.166664568298827e-2)
            + r2 * (np.float32(-1.388731625493765e-3) + r2 * np.float32(2.443315711809948e-5))
        )
    )
    k = n.astype(I32)
    swap = (k & 1) == 1
    sin = jnp.where(swap, c, s)
    cos = jnp.where(swap, s, c)
    sin = jnp.where((k & 2) == 2, -sin, sin)
    cos = jnp.where(((k + 1) & 2) == 2, -cos, cos)
    return sin, cos


def dft_tables():
    turns = ((np.arange(SPOT)[:, None] - SPOT // 2) * np.arange(SUB)[None, :]) % SPOT
    angle = turns * (2.0 * np.pi / SPOT)
    c, s = np.cos(angle), -np.sin(angle)
    cols = np.concatenate([np.kron(np.eye(8), c.T), np.kron(np.eye(8), s.T)], axis=1)
    cb, sb = np.kron(np.eye(2), c), np.kron(np.eye(2), s)
    rows = np.block([[cb, -sb], [sb, cb]])
    cols_hi, cols_lo = halves(cols)
    rows_hi, rows_lo = halves(rows)
    return (
        np.concatenate([cols_hi, cols_lo, cols_hi], axis=0),
        np.concatenate([rows_hi, rows_lo, rows_hi], axis=1),
    )


def halves(a):
    a = a.astype(np.float32)
    hi = a.astype(ml_dtypes.bfloat16)
    return hi, (a - hi.astype(np.float32)).astype(ml_dtypes.bfloat16)


def split(a):
    hi = a.astype(BF16)
    return hi, (a - hi.astype(F32)).astype(BF16)


def shift_at(b, xl, k):
    px = ((b >> 4) * 2 + xl + (k & 3)) & 3
    py = ((b >> 2) + (k >> 2)) & 3
    pz = (b + (k >> 4)) & 3
    return (px >> 1) * 16 + py * 4 + pz, px & 1


def kernel(
    wind, offs, ratio, magic, screens, amp_h,
    new_out, phase, ampn,
    x, amp, send1, recv_a, recv_b, recv_c, side_s, side_r, edge_s, edge_r, y,
    relb, frac, cols, mate_a, mate_b, mate_c, rows_a, rows_b, rows_c, kidx,
    send2a, send2b, recv2a, recv2b, wbig_a, wbig_b,
    in_sem, tab_sem, s1, r1, hs, hr, ws, wr, s2, r2, osem,
):
    recv1 = (recv_a, recv_b, recv_c)
    mate, rows = (mate_a, mate_b, mate_c), (rows_a, rows_b, rows_c)
    b = lax.axis_index("layer")
    q = lax.axis_index("dir")
    xl, c = q // 2, q % 2
    chip = b * 2 + xl

    def device(pb, pxl):
        return (pb, pxl * 2 + c)

    loads = [pltpu.make_async_copy(screens.at[l], x.at[l], in_sem.at[l]) for l in range(LAYERS)]
    for load in loads:
        load.start()

    def block(db, dq):
        return ((b + db) & 31, (q + dq) & 3)

    near = [(db, dq) for db in (-1, 0, 1) for dq in (-1, 1)]
    bar = pltpu.get_barrier_semaphore()
    for n in near:
        pl.semaphore_signal(bar, inc=1, device_id=block(*n), device_id_type=MESH)

    def greet(k, _):
        pl.semaphore_signal(bar, inc=1, device_id=device(*shift_at(b, xl, 64 - k)), device_id_type=MESH)
        return 0

    lax.fori_loop(1, CHIPS, greet, 0)

    amp_load = pltpu.make_async_copy(amp_h, amp, tab_sem)
    amp_load.start()

    ro, ri = iota((BLK, BLK), 0), iota((BLK, BLK), 1)
    perm = jnp.where(ri == (ro & 7) * 64 + (ro >> 3), 1.0, 0.0).astype(BF16)

    def permute(l):
        loads[l].wait()
        ordered = jnp.dot(perm, x[l], preferred_element_type=F32)
        for t in range(4):
            send1[l, :, t] = ordered[:, t * 128:(t + 1) * 128].reshape(CHIPS, 8, 128).astype(BF16)

    def exchange(l):
        def go(k, _):
            pb, pxl = shift_at(b, xl, 64 - k)
            pltpu.make_async_remote_copy(
                src_ref=send1.at[l, pb * 2 + pxl],
                dst_ref=recv1[l].at[xl, pl.ds(b * 4, 4)],
                send_sem=s1.at[l], recv_sem=r1.at[l],
                device_id=device(pb, pxl), device_id_type=MESH,
            ).start()
            return 0

        lax.fori_loop(1, CHIPS, go, 0)
        pltpu.make_async_copy(send1.at[l, chip], recv1[l].at[xl, pl.ds(b * 4, 4)], r1.at[l]).start()

    def sent(l):
        pltpu.make_async_copy(send1.at[l, 0:63], send1.at[l, 0:63], s1.at[l]).wait()

    permute(0)
    pl.semaphore_wait(bar, 63 + len(near))
    exchange(0)
    permute(1)
    permute(2)

    lane8, row8 = iota((8, 128), 1), iota((8, 128), 0)
    first = jnp.where(lane8 == row8, 1.0, 0.0).astype(BF16)
    last = jnp.where(lane8 == row8 + 120, 1.0, 0.0).astype(BF16)
    nt = (((1,), (1,)), ((), ()))
    for l in range(LAYERS):
        side_s[0, l] = lax.dot_general(
            last, x[l, :, BLK - 128:], nt, preferred_element_type=F32).astype(BF16)
        side_s[1, l] = lax.dot_general(
            first, x[l, :, :128], nt, preferred_element_type=F32).astype(BF16)
        edge_s[0, l] = x[l, BLK - 8:]
        edge_s[1, l] = x[l, :8]

    def halo(i, src, dst, to):
        return pltpu.make_async_remote_copy(
            src_ref=src, dst_ref=dst, send_sem=hs.at[i], recv_sem=hr.at[i],
            device_id=to, device_id_type=MESH)

    halos = []
    for i, db in enumerate((1, -1)):
        dst = side_r.at[i]
        halos.append(halo(4 * i, side_s.at[i], dst.at[:, :, 128:128 + BLK], block(db, 0)))
        halos.append(halo(4 * i + 1, side_s.at[i, :, :, BLK - 128:], dst.at[:, :, :128], block(db, 1)))
        halos.append(halo(4 * i + 2, side_s.at[i, :, :, :128], dst.at[:, :, 128 + BLK:], block(db, -1)))
        halos.append(halo(4 * i + 3, edge_s.at[i], edge_r.at[i], block(0, db)))
    for h in halos:
        h.start()

    sent(0)
    exchange(1)

    def row_table(p, _):
        for l in range(LAYERS):
            for pxl in range(2):
                d = pxl * 2 + c
                num, den = ratio[l, 0, d], ratio[l, 1, d]
                r = offs[l, 0, d] - wind[0, l] + ROWS + stretch(p, NPR, num, den, magic[den])
                kidx[l, p * 2 + pxl] = ((r + ((chip - r) & 63)) & (ROWS - 1)) >> 6
        return 0

    lax.fori_loop(0, 32, row_table, 0)
    cols[...] = jnp.zeros_like(cols)

    px0 = (iota((16, 128), 0) * 128).astype(F32)
    px = px0 + iota((16, 128), 1).astype(F32)
    for d in range(DIRS):
        for l in range(LAYERS):
            num = ratio[l, 0, d].astype(F32)
            den = ratio[l, 1, d].astype(F32)
            start = (offs[l, 1, d] - wind[1, l] + COLS) & (COLS - 1)
            a = px * num
            qv = floor_div(a, den)
            tile = (start + floor_div(px0 * num, den).astype(I32)) >> 7
            relb[d * LAYERS + l] = start + qv.astype(I32) - tile * 128
            frac[d * LAYERS + l] = (a - qv * den) / den

    pupil = (b * NPR + iota((NPR, 1), 0)).astype(F32)

    def row_weights(l, mrow):
        num = ratio[l, 0, q].astype(F32)
        den = ratio[l, 1, q].astype(F32)
        start = (offs[l, 0, q] - wind[0, l] + ROWS) & (ROWS - 1)
        a = pupil * num
        qv = floor_div(a, den)
        f = (a - qv * den) / den
        base = (start + qv.astype(I32)) & 63
        high = f.astype(BF16).astype(F32)
        low = (1.0 - f).astype(BF16).astype(F32)
        return jnp.where(mrow == base, low, 0.0) + jnp.where(mrow == ((base + 1) & 63), high, 0.0)

    cc = iota((NPR, CHIPS * 16), 1)
    m, r = cc >> 4, cc & 15
    w0, w1, w2 = [row_weights(l, m) for l in range(LAYERS)]
    wa, wb = jnp.where(r < 10, w0, w1), jnp.where(r < 4, w1, w2)
    for j in range(JT):
        in_a, in_b = r == j, (r == j + 4) & (r >= 4)
        if j < 6:
            in_a = in_a | (r == j + 10)
        else:
            in_b = in_b | (r == j - 6)
        wbig_a[j * NPR:(j + 1) * NPR] = jnp.where(in_a, wa, 0.0).astype(BF16)
        wbig_b[j * NPR:(j + 1) * NPR] = jnp.where(in_b, wb, 0.0).astype(BF16)

    amp_load.wait()
    g32 = jnp.where((iota((32, 32), 0) >> 4) == (iota((32, 32), 1) >> 4), 1.0, 0.0)
    g128 = jnp.where((iota((128, 128), 0) >> 4) == (iota((128, 128), 1) >> 4), 1.0, 0.0)
    for j in range(JT):
        av = amp[:, j * 128:(j + 1) * 128]
        energy = jnp.dot(g32, av * av, precision=HIGHEST, preferred_element_type=F32)
        energy = jnp.dot(energy, g128, precision=HIGHEST, preferred_element_type=F32)
        ampn[j] = av / jnp.sqrt(energy)

    sent(1)
    exchange(2)
    for h in halos:
        h.wait()
    tn = (((0,), (0,)), ((), ()))
    for l in range(LAYERS):
        w0, w1 = wind[0, l], wind[1, l]
        left = lax.dot_general(side_r[0, l], last, tn, preferred_element_type=F32)
        right = lax.dot_general(side_r[1, l], first, tn, preferred_element_type=F32)
        for r0, n, src in ((0, 8, edge_r.at[0, l]), (8, BLK, x.at[l]), (BLK + 8, 8, edge_r.at[1, l])):
            at = r0 + 120
            lanes = [left[at:at + n]]
            lanes += [src[:, t * 128:(t + 1) * 128].astype(F32) for t in range(4)]
            lanes += [right[at:at + n]]
            turned = [pltpu.roll(v, (w1 + 128) & 127, 1) for v in lanes]
            lane = iota((n, 128), 1)
            before, after = lane < w1, lane >= 128 + w1
            for t in range(4):
                y[r0:r0 + n, t * 128:(t + 1) * 128] = jnp.where(
                    before, turned[t], jnp.where(after, turned[t + 2], turned[t + 1]))
        turn, whole = w0 & 7, w0 >> 3
        keep = iota((BLK // 8 + 1, 8, 128), 1) >= turn
        for t in range(4):
            part = y[:, t * 128:(t + 1) * 128].reshape(BLK // 8 + 2, 8, 128)
            part = pltpu.roll(part, turn, 1)
            part = jnp.concatenate([part[:1], jnp.where(keep, part[1:], part[:-1])], axis=0)
            val = jnp.where(whole > 0, part[:-2], jnp.where(whole == 0, part[1:-1], part[2:]))
            x[l, :, t * 128:(t + 1) * 128] = val.reshape(BLK, 128).astype(BF16)
        pltpu.make_async_copy(x.at[l], new_out.at[l], osem.at[l]).start()

    def columns(l):
        def one(d, j):
            num, den = ratio[l, 0, d], ratio[l, 1, d]
            start = (offs[l, 1, d] - wind[1, l] + COLS) & (COLS - 1)
            tile = (start + stretch(j, 128, num, den, magic[den])) >> 7
            rel = relb[d * LAYERS + l, pl.ds(j, 1), :]
            f = frac[d * LAYERS + l, pl.ds(j, 1), :]
            high = f.astype(BF16).astype(F32)
            low = (1.0 - f).astype(BF16).astype(F32)
            rel = jnp.broadcast_to(rel, (8, 128))
            rel_u = rel + 1
            idx, idx_u = rel & 127, rel_u & 127
            sel, sel_u = rel >> 7, rel_u >> 7
            for h in range(2):
                t = [recv1[l][h, (tile + s) & 127].astype(F32) for s in range(3)]
                g = [jnp.take_along_axis(v, idx, axis=1) for v in t]
                u = [jnp.take_along_axis(v, idx_u, axis=1) for v in t]
                vb = jnp.where(sel == 0, g[0], jnp.where(sel == 1, g[1], g[2]))
                vu = jnp.where(sel_u == 0, u[0], jnp.where(sel_u == 1, u[1], u[2]))
                out = low * vb + high * vu
                cols.at[d % 2, d // 2, h].reshape(128, 128)[pl.ds(j, 8, stride=16), :] = out

        def toward(core):
            def direction(i, _):
                for j in range(JT):
                    one(2 * i + core, j)
                return 0

            lax.fori_loop(0, 2, direction, 0)

        toward(1 - c)
        mate[l][...] = cols[1 - c].astype(BF16)
        swap(l).start()
        toward(c)
        rows[l][c] = cols[c].astype(BF16)

    def swap(l):
        return pltpu.make_async_remote_copy(
            src_ref=mate[l], dst_ref=rows[l].at[c],
            send_sem=ws.at[l], recv_sem=wr.at[l],
            device_id=(b, xl * 2 + 1 - c), device_id_type=MESH)

    def arrive(l):
        pltpu.make_async_copy(recv1[l], recv1[l], r1.at[l]).wait()
        columns(l)

    def row_of(l, dest):
        k = kidx[l, dest]
        return rows[l][(k >> 3) & 1, dest & 1, k >> 4, k & 7]

    sub = iota((8, 128), 0)

    def turn_rows(v, n):
        return pltpu.roll(v[:8], n, 0), pltpu.roll(v[8:], n, 0)

    def pack_a(dest):
        a, b0 = row_of(0, dest).astype(F32), row_of(1, dest).astype(F32)
        t0, _ = turn_rows(b0, 2)
        send2a[dest] = jnp.concatenate([a[:8], jnp.where(sub < 2, a[8:], t0)], axis=0).astype(BF16)

    def pack_b(dest):
        t0, t1 = turn_rows(row_of(1, dest).astype(F32), 2)
        u0, u1 = turn_rows(row_of(2, dest).astype(F32), 4)
        top = jnp.where(sub < 2, t0, jnp.where(sub < 4, t1, u0))
        send2b[dest] = jnp.concatenate([top, jnp.where(sub < 4, u0, u1)], axis=0).astype(BF16)

    def deliver(i, src, dst, pack):
        def some(n, _):
            for u in range(7):
                pb, pxl = shift_at(b, xl, 63 - n * 7 - u)
                pack(pb * 2 + pxl)
            for u in range(7):
                pb, pxl = shift_at(b, xl, 63 - n * 7 - u)
                pltpu.make_async_remote_copy(
                    src_ref=src.at[pb * 2 + pxl], dst_ref=dst.at[chip],
                    send_sem=s2.at[i], recv_sem=r2.at[i * (1 + (chip >> 4))],
                    device_id=device(pb, pxl), device_id_type=MESH,
                ).start()
            return 0

        lax.fori_loop(0, 9, some, 0)
        pack(chip)
        pltpu.make_async_copy(src.at[chip], dst.at[chip], r2.at[i * (1 + (chip >> 4))]).start()

    arrive(0)
    arrive(1)
    swap(0).wait()
    swap(1).wait()
    deliver(0, send2a, recv2a, pack_a)
    arrive(2)
    swap(2).wait()
    deliver(1, send2b, recv2b, pack_b)

    pltpu.make_async_copy(recv2a, recv2a, r2.at[0]).wait()
    phase[...] = jnp.dot(
        wbig_a[...], recv2a[...].reshape(CHIPS * 16, 128), preferred_element_type=F32)
    total = phase[...]
    for n in range(4):
        part = recv2b.at[n * 16:(n + 1) * 16]
        pltpu.make_async_copy(part, part, r2.at[1 + n]).wait()
        total = total + jnp.dot(
            wbig_b[:, n * 256:(n + 1) * 256], part[...].reshape(256, 128), preferred_element_type=F32)
    phase[...] = total

    for l in range(LAYERS):
        pltpu.make_async_copy(x.at[l], new_out.at[l], osem.at[l]).wait()
    sent(2)
    pltpu.make_async_copy(send2a.at[0:63], send2a.at[0:63], s2.at[0]).wait()
    pltpu.make_async_copy(send2b.at[0:63], send2b.at[0:63], s2.at[1]).wait()


def image(phase, ampn, dcol, drow, new_in, new_out, spots, field, half, out, nsem, osem):
    copy = pltpu.make_async_copy(new_in, new_out, nsem)
    copy.start()
    for j in range(JT):
        sin, cos = sincos(phase[j * NPR:(j + 1) * NPR])
        for i, v in enumerate((ampn[j] * cos, ampn[j] * sin)):
            hi, lo = split(v)
            at = j * 64 + i * 32
            field[at:at + 32, :128] = hi
            field[at:at + 32, 128:256] = hi
            field[at:at + 32, 256:] = lo
    half[...] = jnp.dot(field[...], dcol[...], preferred_element_type=F32)
    stores = []
    for j in range(JT):
        g = half[j * 64:(j + 1) * 64]
        re = split(g[:32, :256] - g[32:, 256:])
        im = split(g[:32, 256:] + g[32:, :256])
        data = jnp.concatenate([re[0], im[0], re[0], im[0], re[1], im[1]], axis=0)
        full = jnp.dot(drow[...], data, preferred_element_type=F32)
        out[:, j * 256:(j + 1) * 256] = full[:64] * full[:64] + full[64:] * full[64:]
        store = pltpu.make_async_copy(
            out.at[:, j * 256:(j + 1) * 256], spots.at[:, j * 256:(j + 1) * 256], osem.at[j])
        store.start()
        stores.append(store)
    for store in stores:
        store.wait()
    copy.wait()


def per_device(screens, amplitude, wind, offsets, ratio):
    dcol, drow = dft_tables()
    vmem = pl.BlockSpec(memory_space=pltpu.VMEM)
    smem = pl.BlockSpec(memory_space=pltpu.SMEM)
    hbm = pl.BlockSpec(memory_space=pltpu.HBM)
    anywhere = pl.BlockSpec(memory_space=pl.ANY)
    dma = pltpu.SemaphoreType.DMA
    new, phase, ampn = pl.pallas_call(
        kernel,
        out_shape=(
            jax.ShapeDtypeStruct((LAYERS, BLK, BLK), BF16),
            jax.ShapeDtypeStruct((JT * NPR, 128), F32),
            jax.ShapeDtypeStruct((JT, NPR, 128), F32),
        ),
        in_specs=[smem, smem, smem, smem, hbm, hbm],
        out_specs=(anywhere, vmem, vmem),
        scratch_shapes=[
            pltpu.VMEM((LAYERS, BLK, BLK), BF16),
            pltpu.VMEM((NPR, PC), F32),
            pltpu.VMEM((LAYERS, CHIPS, 4, 8, 128), BF16),
            pltpu.VMEM((2, 128, 8, 128), BF16),
            pltpu.VMEM((2, 128, 8, 128), BF16),
            pltpu.VMEM((2, 128, 8, 128), BF16),
            pltpu.VMEM((2, LAYERS, 8, BLK), BF16),
            pltpu.VMEM((2, LAYERS, 8, BLK + 256), BF16),
            pltpu.VMEM((2, LAYERS, 8, BLK), BF16),
            pltpu.VMEM((2, LAYERS, 8, BLK), BF16),
            pltpu.VMEM((BLK + 16, BLK), F32),
            pltpu.VMEM((DIRS * LAYERS, 16, 128), I32),
            pltpu.VMEM((DIRS * LAYERS, 16, 128), F32),
            pltpu.VMEM((2, 2, 2, 8, 16, 128), F32),
            *[pltpu.VMEM((2, 2, 8, 16, 128), BF16)] * 3,
            *[pltpu.VMEM((2, 2, 2, 8, 16, 128), BF16)] * 3,
            pltpu.SMEM((LAYERS, CHIPS), I32),
            pltpu.VMEM((CHIPS, 16, 128), BF16),
            pltpu.VMEM((CHIPS, 16, 128), BF16),
            pltpu.VMEM((CHIPS, 16, 128), BF16),
            pltpu.VMEM((CHIPS, 16, 128), BF16),
            pltpu.VMEM((JT * NPR, CHIPS * 16), BF16),
            pltpu.VMEM((JT * NPR, CHIPS * 16), BF16),
            dma((3,)), dma, dma((3,)), dma((3,)), dma((8,)), dma((8,)),
            dma((3,)), dma((3,)), dma((2,)), dma((5,)), dma((3,)),
        ],
        compiler_params=pltpu.CompilerParams(
            collective_id=0, has_side_effects=True, vmem_limit_bytes=32 << 20),
        name="screens_to_phase",
    )(
        *[
            pltpu.with_memory_space_constraint(v, pltpu.HBM)
            for v in (
                wind.T, offsets.transpose(1, 2, 0), ratio.transpose(1, 2, 0),
                jnp.asarray(reciprocals()), screens, amplitude,
            )
        ]
    )
    new, spots = pl.pallas_call(
        image,
        out_shape=(
            jax.ShapeDtypeStruct((LAYERS, BLK, BLK), BF16),
            jax.ShapeDtypeStruct((64, 2560), F32),
        ),
        in_specs=[vmem, vmem, vmem, vmem, anywhere],
        out_specs=(hbm, hbm),
        scratch_shapes=[
            pltpu.VMEM((JT * 64, 384), BF16),
            pltpu.VMEM((JT * 64, 512), F32),
            pltpu.VMEM((64, 2560), F32),
            dma, dma((JT,)),
        ],
        compiler_params=pltpu.CompilerParams(vmem_limit_bytes=32 << 20),
        name="phase_to_spots",
    )(phase, ampn, jnp.asarray(dcol), jnp.asarray(drow), new)
    return new, spots[None]


def solution(mesh):
    return jax.shard_map(
        per_device,
        mesh=mesh,
        in_specs=(P(None, "dir", "layer"), P("layer", None), P(), P(), P()),
        out_specs=(P(None, "dir", "layer"), P("dir", "layer", None)),
        check_vma=False,
    )
```

```python
import jax
import jax.numpy as jnp
import ml_dtypes
import numpy as np
from jax import lax
from jax.experimental import pallas as pl
from jax.experimental.pallas import tpu as pltpu
from jax.sharding import PartitionSpec as P

MESH = pl.DeviceIdType.MESH
SUB = 16
SPOT = 32
HALO = 8
LAYERS = 3
DIRS = 4
ROWS, COLS = 2048, 16384
PR, PC = 1024, 1280
BLK = 512
CHIPS = 64
JT = PC // 128
NPR = 32
F32, BF16, I32 = jnp.float32, jnp.bfloat16, jnp.int32
HIGHEST = lax.Precision.HIGHEST


def iota(shape, dim):
    return lax.broadcasted_iota(I32, shape, dim)


def floor_div(a, den):
    q = jnp.floor(a / den)
    r = a - q * den
    q = q + jnp.where(r >= den, 1.0, 0.0) - jnp.where(r < 0.0, 1.0, 0.0)
    return q


def reciprocals():
    den = np.maximum(np.arange(129), 1)
    return (2 ** 21 // den + 1).astype(np.int32)


def stretch(i, unit, num, den, mul):
    part = i * (num - den)
    whole = (part * mul) >> 21
    rest = part - whole * den
    return unit * (i + whole) + ((unit * rest * mul) >> 21)


def sincos(x):
    n = jnp.floor(x * np.float32(2.0 / np.pi) + 0.5)
    r = x - n * np.float32(1.5703125)
    r = r - n * np.float32(4.837512969970703125e-4)
    r = r - n * np.float32(7.54978995489188216e-8)
    r2 = r * r
    s = r + r * r2 * (
        np.float32(-1.6666654611e-1)
        + r2 * (np.float32(8.3321608736e-3) + r2 * np.float32(-1.9515295891e-4))
    )
    c = (
        1.0
        - 0.5 * r2
        + r2 * r2 * (
            np.float32(4.166664568298827e-2)
            + r2 * (np.float32(-1.388731625493765e-3) + r2 * np.float32(2.443315711809948e-5))
        )
    )
    k = n.astype(I32)
    swap = (k & 1) == 1
    sin = jnp.where(swap, c, s)
    cos = jnp.where(swap, s, c)
    sin = jnp.where((k & 2) == 2, -sin, sin)
    cos = jnp.where(((k + 1) & 2) == 2, -cos, cos)
    return sin, cos


def dft_tables():
    turns = ((np.arange(SPOT)[:, None] - SPOT // 2) * np.arange(SUB)[None, :]) % SPOT
    angle = turns * (2.0 * np.pi / SPOT)
    c, s = np.cos(angle), -np.sin(angle)
    cols = np.concatenate([np.kron(np.eye(8), c.T), np.kron(np.eye(8), s.T)], axis=1)
    cb, sb = np.kron(np.eye(2), c), np.kron(np.eye(2), s)
    rows = np.block([[cb, -sb], [sb, cb]])
    cols_hi, cols_lo = halves(cols)
    rows_hi, rows_lo = halves(rows)
    return (
        np.concatenate([cols_hi, cols_lo, cols_hi], axis=0),
        np.concatenate([rows_hi, rows_lo, rows_hi], axis=1),
    )


def halves(a):
    a = a.astype(np.float32)
    hi = a.astype(ml_dtypes.bfloat16)
    return hi, (a - hi.astype(np.float32)).astype(ml_dtypes.bfloat16)


def split(a):
    hi = a.astype(BF16)
    return hi, (a - hi.astype(F32)).astype(BF16)


def shift_at(b, xl, k):
    px = ((b >> 4) * 2 + xl + (k & 3)) & 3
    py = ((b >> 2) + (k >> 2)) & 3
    pz = (b + (k >> 4)) & 3
    return (px >> 1) * 16 + py * 4 + pz, px & 1


def kernel(
    wind, offs, ratio, magic, screens, amp_h,
    new_out, phase, ampn,
    x, amp, send1, recv_a, recv_b, recv_c, side_s, side_r, edge_s, edge_r, y,
    relb, frac, cols, mate_a, mate_b, mate_c, rows_a, rows_b, rows_c, kidx,
    send2a, send2b, recv2a, recv2b, wbig_a, wbig_b,
    in_sem, tab_sem, s1, r1, hs, hr, ws, wr, s2, r2, osem,
):
    recv1 = (recv_a, recv_b, recv_c)
    mate, rows = (mate_a, mate_b, mate_c), (rows_a, rows_b, rows_c)
    b = lax.axis_index("layer")
    q = lax.axis_index("dir")
    xl, c = q // 2, q % 2
    chip = b * 2 + xl

    def device(pb, pxl):
        return (pb, pxl * 2 + c)

    loads = [pltpu.make_async_copy(screens.at[l], x.at[l], in_sem.at[l]) for l in range(LAYERS)]
    for load in loads:
        load.start()

    def block(db, dq):
        return ((b + db) & 31, (q + dq) & 3)

    near = [(db, dq) for db in (-1, 0, 1) for dq in (-1, 1)]
    bar = pltpu.get_barrier_semaphore()
    for n in near:
        pl.semaphore_signal(bar, inc=1, device_id=block(*n), device_id_type=MESH)

    def greet(k, _):
        pl.semaphore_signal(bar, inc=1, device_id=device(*shift_at(b, xl, 64 - k)), device_id_type=MESH)
        return 0

    lax.fori_loop(1, CHIPS, greet, 0)

    amp_load = pltpu.make_async_copy(amp_h, amp, tab_sem)
    amp_load.start()

    ro, ri = iota((BLK, BLK), 0), iota((BLK, BLK), 1)
    perm = jnp.where(ri == (ro & 7) * 64 + (ro >> 3), 1.0, 0.0).astype(BF16)

    def permute(l):
        loads[l].wait()
        ordered = jnp.dot(perm, x[l], preferred_element_type=F32)
        for t in range(4):
            send1[l, :, t] = ordered[:, t * 128:(t + 1) * 128].reshape(CHIPS, 8, 128).astype(BF16)

    def exchange(l):
        def go(k, _):
            pb, pxl = shift_at(b, xl, 64 - k)
            pltpu.make_async_remote_copy(
                src_ref=send1.at[l, pb * 2 + pxl],
                dst_ref=recv1[l].at[xl, pl.ds(b * 4, 4)],
                send_sem=s1.at[l], recv_sem=r1.at[l],
                device_id=device(pb, pxl), device_id_type=MESH,
            ).start()
            return 0

        lax.fori_loop(1, CHIPS, go, 0)
        pltpu.make_async_copy(send1.at[l, chip], recv1[l].at[xl, pl.ds(b * 4, 4)], r1.at[l]).start()

    def sent(l):
        pltpu.make_async_copy(send1.at[l, 0:63], send1.at[l, 0:63], s1.at[l]).wait()

    permute(0)
    pl.semaphore_wait(bar, 63 + len(near))
    exchange(0)
    permute(1)
    permute(2)

    lane8, row8 = iota((8, 128), 1), iota((8, 128), 0)
    first = jnp.where(lane8 == row8, 1.0, 0.0).astype(BF16)
    last = jnp.where(lane8 == row8 + 120, 1.0, 0.0).astype(BF16)
    nt = (((1,), (1,)), ((), ()))
    for l in range(LAYERS):
        side_s[0, l] = lax.dot_general(
            last, x[l, :, BLK - 128:], nt, preferred_element_type=F32).astype(BF16)
        side_s[1, l] = lax.dot_general(
            first, x[l, :, :128], nt, preferred_element_type=F32).astype(BF16)
        edge_s[0, l] = x[l, BLK - 8:]
        edge_s[1, l] = x[l, :8]

    def halo(i, src, dst, to):
        return pltpu.make_async_remote_copy(
            src_ref=src, dst_ref=dst, send_sem=hs.at[i], recv_sem=hr.at[i],
            device_id=to, device_id_type=MESH)

    halos = []
    for i, db in enumerate((1, -1)):
        dst = side_r.at[i]
        halos.append(halo(4 * i, side_s.at[i], dst.at[:, :, 128:128 + BLK], block(db, 0)))
        halos.append(halo(4 * i + 1, side_s.at[i, :, :, BLK - 128:], dst.at[:, :, :128], block(db, 1)))
        halos.append(halo(4 * i + 2, side_s.at[i, :, :, :128], dst.at[:, :, 128 + BLK:], block(db, -1)))
        halos.append(halo(4 * i + 3, edge_s.at[i], edge_r.at[i], block(0, db)))
    for h in halos:
        h.start()

    sent(0)
    exchange(1)

    def row_table(p, _):
        for l in range(LAYERS):
            for pxl in range(2):
                d = pxl * 2 + c
                num, den = ratio[l, 0, d], ratio[l, 1, d]
                r = offs[l, 0, d] - wind[0, l] + ROWS + stretch(p, NPR, num, den, magic[den])
                kidx[l, p * 2 + pxl] = ((r + ((chip - r) & 63)) & (ROWS - 1)) >> 6
        return 0

    lax.fori_loop(0, 32, row_table, 0)
    cols[...] = jnp.zeros_like(cols)

    px0 = (iota((16, 128), 0) * 128).astype(F32)
    px = px0 + iota((16, 128), 1).astype(F32)
    for d in range(DIRS):
        for l in range(LAYERS):
            num = ratio[l, 0, d].astype(F32)
            den = ratio[l, 1, d].astype(F32)
            start = (offs[l, 1, d] - wind[1, l] + COLS) & (COLS - 1)
            a = px * num
            qv = floor_div(a, den)
            tile = (start + floor_div(px0 * num, den).astype(I32)) >> 7
            relb[d * LAYERS + l] = start + qv.astype(I32) - tile * 128
            frac[d * LAYERS + l] = (a - qv * den) / den

    pupil = (b * NPR + iota((NPR, 1), 0)).astype(F32)

    def row_weights(l, mrow):
        num = ratio[l, 0, q].astype(F32)
        den = ratio[l, 1, q].astype(F32)
        start = (offs[l, 0, q] - wind[0, l] + ROWS) & (ROWS - 1)
        a = pupil * num
        qv = floor_div(a, den)
        f = (a - qv * den) / den
        base = (start + qv.astype(I32)) & 63
        high = f.astype(BF16).astype(F32)
        low = (1.0 - f).astype(BF16).astype(F32)
        return jnp.where(mrow == base, low, 0.0) + jnp.where(mrow == ((base + 1) & 63), high, 0.0)

    cc = iota((NPR, CHIPS * 16), 1)
    m, r = cc >> 4, cc & 15
    w0, w1, w2 = [row_weights(l, m) for l in range(LAYERS)]
    wa, wb = jnp.where(r < 10, w0, w1), jnp.where(r < 4, w1, w2)
    for j in range(JT):
        in_a, in_b = r == j, (r == j + 4) & (r >= 4)
        if j < 6:
            in_a = in_a | (r == j + 10)
        else:
            in_b = in_b | (r == j - 6)
        wbig_a[j * NPR:(j + 1) * NPR] = jnp.where(in_a, wa, 0.0).astype(BF16)
        wbig_b[j * NPR:(j + 1) * NPR] = jnp.where(in_b, wb, 0.0).astype(BF16)

    amp_load.wait()
    g32 = jnp.where((iota((32, 32), 0) >> 4) == (iota((32, 32), 1) >> 4), 1.0, 0.0)
    g128 = jnp.where((iota((128, 128), 0) >> 4) == (iota((128, 128), 1) >> 4), 1.0, 0.0)
    for j in range(JT):
        av = amp[:, j * 128:(j + 1) * 128]
        energy = jnp.dot(g32, av * av, precision=HIGHEST, preferred_element_type=F32)
        energy = jnp.dot(energy, g128, precision=HIGHEST, preferred_element_type=F32)
        ampn[j] = av / jnp.sqrt(energy)

    sent(1)
    exchange(2)
    for h in halos:
        h.wait()
    tn = (((0,), (0,)), ((), ()))
    for l in range(LAYERS):
        w0, w1 = wind[0, l], wind[1, l]
        left = lax.dot_general(side_r[0, l], last, tn, preferred_element_type=F32)
        right = lax.dot_general(side_r[1, l], first, tn, preferred_element_type=F32)
        for r0, n, src in ((0, 8, edge_r.at[0, l]), (8, BLK, x.at[l]), (BLK + 8, 8, edge_r.at[1, l])):
            at = r0 + 120
            lanes = [left[at:at + n]]
            lanes += [src[:, t * 128:(t + 1) * 128].astype(F32) for t in range(4)]
            lanes += [right[at:at + n]]
            turned = [pltpu.roll(v, (w1 + 128) & 127, 1) for v in lanes]
            lane = iota((n, 128), 1)
            before, after = lane < w1, lane >= 128 + w1
            for t in range(4):
                y[r0:r0 + n, t * 128:(t + 1) * 128] = jnp.where(
                    before, turned[t], jnp.where(after, turned[t + 2], turned[t + 1]))
        turn, whole = w0 & 7, w0 >> 3
        keep = iota((BLK // 8 + 1, 8, 128), 1) >= turn
        for t in range(4):
            part = y[:, t * 128:(t + 1) * 128].reshape(BLK // 8 + 2, 8, 128)
            part = pltpu.roll(part, turn, 1)
            part = jnp.concatenate([part[:1], jnp.where(keep, part[1:], part[:-1])], axis=0)
            val = jnp.where(whole > 0, part[:-2], jnp.where(whole == 0, part[1:-1], part[2:]))
            x[l, :, t * 128:(t + 1) * 128] = val.reshape(BLK, 128).astype(BF16)
        pltpu.make_async_copy(x.at[l], new_out.at[l], osem.at[l]).start()

    def columns(l):
        def one(d, j):
            num, den = ratio[l, 0, d], ratio[l, 1, d]
            start = (offs[l, 1, d] - wind[1, l] + COLS) & (COLS - 1)
            tile = (start + stretch(j, 128, num, den, magic[den])) >> 7
            rel = relb[d * LAYERS + l, pl.ds(j, 1), :]
            f = frac[d * LAYERS + l, pl.ds(j, 1), :]
            high = f.astype(BF16).astype(F32)
            low = (1.0 - f).astype(BF16).astype(F32)
            rel = jnp.broadcast_to(rel, (8, 128))
            rel_u = rel + 1
            idx, idx_u = rel & 127, rel_u & 127
            sel, sel_u = rel >> 7, rel_u >> 7
            for h in range(2):
                t = [recv1[l][h, (tile + s) & 127].astype(F32) for s in range(3)]
                g = [jnp.take_along_axis(v, idx, axis=1) for v in t]
                u = [jnp.take_along_axis(v, idx_u, axis=1) for v in t]
                vb = jnp.where(sel == 0, g[0], jnp.where(sel == 1, g[1], g[2]))
                vu = jnp.where(sel_u == 0, u[0], jnp.where(sel_u == 1, u[1], u[2]))
                out = low * vb + high * vu
                cols.at[d % 2, d // 2, h].reshape(128, 128)[pl.ds(j, 8, stride=16), :] = out

        def toward(core):
            def direction(i, _):
                for j in range(JT):
                    one(2 * i + core, j)
                return 0

            lax.fori_loop(0, 2, direction, 0)

        toward(1 - c)
        mate[l][...] = cols[1 - c].astype(BF16)
        swap(l).start()
        toward(c)
        rows[l][c] = cols[c].astype(BF16)

    def swap(l):
        return pltpu.make_async_remote_copy(
            src_ref=mate[l], dst_ref=rows[l].at[c],
            send_sem=ws.at[l], recv_sem=wr.at[l],
            device_id=(b, xl * 2 + 1 - c), device_id_type=MESH)

    def arrive(l):
        pltpu.make_async_copy(recv1[l], recv1[l], r1.at[l]).wait()
        columns(l)

    def row_of(l, dest):
        k = kidx[l, dest]
        return rows[l][(k >> 3) & 1, dest & 1, k >> 4, k & 7]

    sub = iota((8, 128), 0)

    def turn_rows(v, n):
        return pltpu.roll(v[:8], n, 0), pltpu.roll(v[8:], n, 0)

    def pack_a(dest):
        a, b0 = row_of(0, dest).astype(F32), row_of(1, dest).astype(F32)
        t0, _ = turn_rows(b0, 2)
        send2a[dest] = jnp.concatenate([a[:8], jnp.where(sub < 2, a[8:], t0)], axis=0).astype(BF16)

    def pack_b(dest):
        t0, t1 = turn_rows(row_of(1, dest).astype(F32), 2)
        u0, u1 = turn_rows(row_of(2, dest).astype(F32), 4)
        top = jnp.where(sub < 2, t0, jnp.where(sub < 4, t1, u0))
        send2b[dest] = jnp.concatenate([top, jnp.where(sub < 4, u0, u1)], axis=0).astype(BF16)

    def deliver(i, src, dst, pack):
        def some(n, _):
            for u in range(3):
                pb, pxl = shift_at(b, xl, 63 - n * 3 - u)
                pack(pb * 2 + pxl)
            for u in range(3):
                pb, pxl = shift_at(b, xl, 63 - n * 3 - u)
                pltpu.make_async_remote_copy(
                    src_ref=src.at[pb * 2 + pxl], dst_ref=dst.at[chip],
                    send_sem=s2.at[i], recv_sem=r2.at[i * (1 + (chip >> 4))],
                    device_id=device(pb, pxl), device_id_type=MESH,
                ).start()
            return 0

        lax.fori_loop(0, 21, some, 0)
        pack(chip)
        pltpu.make_async_copy(src.at[chip], dst.at[chip], r2.at[i * (1 + (chip >> 4))]).start()

    arrive(0)
    arrive(1)
    swap(0).wait()
    swap(1).wait()
    deliver(0, send2a, recv2a, pack_a)
    arrive(2)
    swap(2).wait()
    deliver(1, send2b, recv2b, pack_b)

    pltpu.make_async_copy(recv2a, recv2a, r2.at[0]).wait()
    phase[...] = jnp.dot(
        wbig_a[...], recv2a[...].reshape(CHIPS * 16, 128), preferred_element_type=F32)
    total = phase[...]
    for n in range(4):
        part = recv2b.at[n * 16:(n + 1) * 16]
        pltpu.make_async_copy(part, part, r2.at[1 + n]).wait()
        total = total + jnp.dot(
            wbig_b[:, n * 256:(n + 1) * 256], part[...].reshape(256, 128), preferred_element_type=F32)
    phase[...] = total

    for l in range(LAYERS):
        pltpu.make_async_copy(x.at[l], new_out.at[l], osem.at[l]).wait()
    sent(2)
    pltpu.make_async_copy(send2a.at[0:63], send2a.at[0:63], s2.at[0]).wait()
    pltpu.make_async_copy(send2b.at[0:63], send2b.at[0:63], s2.at[1]).wait()


def image(phase, ampn, dcol, drow, new_in, new_out, spots, field, half, out, nsem, osem):
    copy = pltpu.make_async_copy(new_in, new_out, nsem)
    copy.start()
    for j in range(JT):
        sin, cos = sincos(phase[j * NPR:(j + 1) * NPR])
        for i, v in enumerate((ampn[j] * cos, ampn[j] * sin)):
            hi, lo = split(v)
            at = j * 64 + i * 32
            field[at:at + 32, :128] = hi
            field[at:at + 32, 128:256] = hi
            field[at:at + 32, 256:] = lo
    half[...] = jnp.dot(field[...], dcol[...], preferred_element_type=F32)
    stores = []
    for j in range(JT):
        g = half[j * 64:(j + 1) * 64]
        re = split(g[:32, :256] - g[32:, 256:])
        im = split(g[:32, 256:] + g[32:, :256])
        data = jnp.concatenate([re[0], im[0], re[0], im[0], re[1], im[1]], axis=0)
        full = jnp.dot(drow[...], data, preferred_element_type=F32)
        out[:, j * 256:(j + 1) * 256] = full[:64] * full[:64] + full[64:] * full[64:]
        store = pltpu.make_async_copy(
            out.at[:, j * 256:(j + 1) * 256], spots.at[:, j * 256:(j + 1) * 256], osem.at[j])
        store.start()
        stores.append(store)
    for store in stores:
        store.wait()
    copy.wait()


def per_device(screens, amplitude, wind, offsets, ratio):
    dcol, drow = dft_tables()
    vmem = pl.BlockSpec(memory_space=pltpu.VMEM)
    smem = pl.BlockSpec(memory_space=pltpu.SMEM)
    hbm = pl.BlockSpec(memory_space=pltpu.HBM)
    anywhere = pl.BlockSpec(memory_space=pl.ANY)
    dma = pltpu.SemaphoreType.DMA
    new, phase, ampn = pl.pallas_call(
        kernel,
        out_shape=(
            jax.ShapeDtypeStruct((LAYERS, BLK, BLK), BF16),
            jax.ShapeDtypeStruct((JT * NPR, 128), F32),
            jax.ShapeDtypeStruct((JT, NPR, 128), F32),
        ),
        in_specs=[smem, smem, smem, smem, hbm, hbm],
        out_specs=(anywhere, vmem, vmem),
        scratch_shapes=[
            pltpu.VMEM((LAYERS, BLK, BLK), BF16),
            pltpu.VMEM((NPR, PC), F32),
            pltpu.VMEM((LAYERS, CHIPS, 4, 8, 128), BF16),
            pltpu.VMEM((2, 128, 8, 128), BF16),
            pltpu.VMEM((2, 128, 8, 128), BF16),
            pltpu.VMEM((2, 128, 8, 128), BF16),
            pltpu.VMEM((2, LAYERS, 8, BLK), BF16),
            pltpu.VMEM((2, LAYERS, 8, BLK + 256), BF16),
            pltpu.VMEM((2, LAYERS, 8, BLK), BF16),
            pltpu.VMEM((2, LAYERS, 8, BLK), BF16),
            pltpu.VMEM((BLK + 16, BLK), F32),
            pltpu.VMEM((DIRS * LAYERS, 16, 128), I32),
            pltpu.VMEM((DIRS * LAYERS, 16, 128), F32),
            pltpu.VMEM((2, 2, 2, 8, 16, 128), F32),
            *[pltpu.VMEM((2, 2, 8, 16, 128), BF16)] * 3,
            *[pltpu.VMEM((2, 2, 2, 8, 16, 128), BF16)] * 3,
            pltpu.SMEM((LAYERS, CHIPS), I32),
            pltpu.VMEM((CHIPS, 16, 128), BF16),
            pltpu.VMEM((CHIPS, 16, 128), BF16),
            pltpu.VMEM((CHIPS, 16, 128), BF16),
            pltpu.VMEM((CHIPS, 16, 128), BF16),
            pltpu.VMEM((JT * NPR, CHIPS * 16), BF16),
            pltpu.VMEM((JT * NPR, CHIPS * 16), BF16),
            dma((3,)), dma, dma((3,)), dma((3,)), dma((8,)), dma((8,)),
            dma((3,)), dma((3,)), dma((2,)), dma((5,)), dma((3,)),
        ],
        compiler_params=pltpu.CompilerParams(
            collective_id=0, has_side_effects=True, vmem_limit_bytes=32 << 20),
        name="screens_to_phase",
    )(
        *[
            pltpu.with_memory_space_constraint(v, pltpu.HBM)
            for v in (
                wind.T, offsets.transpose(1, 2, 0), ratio.transpose(1, 2, 0),
                jnp.asarray(reciprocals()), screens, amplitude,
            )
        ]
    )
    new, spots = pl.pallas_call(
        image,
        out_shape=(
            jax.ShapeDtypeStruct((LAYERS, BLK, BLK), BF16),
            jax.ShapeDtypeStruct((64, 2560), F32),
        ),
        in_specs=[vmem, vmem, vmem, vmem, anywhere],
        out_specs=(hbm, hbm),
        scratch_shapes=[
            pltpu.VMEM((JT * 64, 384), BF16),
            pltpu.VMEM((JT * 64, 512), F32),
            pltpu.VMEM((64, 2560), F32),
            dma, dma((JT,)),
        ],
        compiler_params=pltpu.CompilerParams(vmem_limit_bytes=32 << 20),
        name="phase_to_spots",
    )(phase, ampn, jnp.asarray(dcol), jnp.asarray(drow), new)
    return new, spots[None]


def solution(mesh):
    return jax.shard_map(
        per_device,
        mesh=mesh,
        in_specs=(P(None, "dir", "layer"), P("layer", None), P(), P(), P()),
        out_specs=(P(None, "dir", "layer"), P("dir", "layer", None)),
        check_vma=False,
    )
```
